256 devices in a mesh: row: 16 (over z, core), col: 16 (over y, x).
Axes of the slice: x: 4, y: 4, z: 8, core: 2. Of those that a mesh axis runs over, the one named last changes fastest.
Arguments:
- inverse: float32 [5, 16, 5, 16, 256, 256], P(None, 'row', None, 'col')
- struct_first: int32 [32], replicated, may hold values from 0 to 79, as said below
- struct_second: int32 [16], replicated, may hold values from 0 to 79, as said below
- factor_first: float32 [32, 256, 256], P('row'), may hold values from -0.25 to 0.25
- factor_second: float32 [16, 256, 256], P('row'), may hold values from -0.25 to 0.25
- link_factor: float32 [256, 256], replicated, may hold values from -0.375 to 0.375
- dinv_first: float32 [256, 256], replicated, may hold values from -6 to 6
- dinv_second: float32 [256, 256], replicated, may hold values from -6 to 6
Outputs:
- column_first: float32 [5, 16, 256, 256], P(None, 'row', None, 'col')
- diag_first: float32 [256, 256], P(None, 'col')
- column_second: float32 [5, 16, 256, 256], P(None, 'row', None, 'col')
- link_second: float32 [256, 256], P(None, 'col')
- diag_second: float32 [256, 256], P(None, 'col')
The draws below stay inside these ranges and needn't reach their ends.
Inputs may be any that keep to these rules, and one draw needn't show every extreme that they name: `struct_first`: distinct tile ids. `struct_second`: distinct tile ids, each of them also in struct_first.
All inputs are finite; a program needn't handle non-finite values.
Results may differ from the reference program's by a relative error of at most 0.0001.
Values sent between devices are 32-bit elements; how exact they have to be, the bound alone decides.
A program may use at most 128 MiB of HBM per device.

```python
import jax
import jax.numpy as jnp
from jax import lax

TILE = 256
ANC_TILES = 80
LIST = 32
LIST2 = 16
N_ROW = 16
N_COL = 16


def structure(key):
    middle = 1 + jax.random.permutation(jax.random.fold_in(key, 11), ANC_TILES - 2)[:LIST - 2].astype(jnp.int32)
    ends = jnp.array([0, ANC_TILES - 1], jnp.int32)
    first = jnp.concatenate([ends, middle])[jax.random.permutation(jax.random.fold_in(key, 12), LIST)]
    second = jnp.concatenate([ends, middle[:LIST2 - 2]])[jax.random.permutation(jax.random.fold_in(key, 13), LIST2)]
    return (first.astype(jnp.int32), second.astype(jnp.int32))


def draw_struct_first(key, part):
    return structure(key)[0]


def draw_struct_second(key, part):
    return structure(key)[1]


def draw_inverse(key, part):
    shape = (ANC_TILES // N_ROW, N_ROW, ANC_TILES // N_COL, N_COL, TILE, TILE)
    spread = (LIST * TILE) ** (-0.5)
    noise = jax.random.normal(key, shape, jnp.float32)
    row_tile = (jnp.arange(ANC_TILES // N_ROW, dtype=jnp.int32)[:, None] * N_ROW + jnp.arange(N_ROW, dtype=jnp.int32)[None, :]).reshape(ANC_TILES // N_ROW, N_ROW, 1, 1, 1, 1)
    col_tile = (jnp.arange(ANC_TILES // N_COL, dtype=jnp.int32)[:, None] * N_COL + jnp.arange(N_COL, dtype=jnp.int32)[None, :]).reshape(1, 1, ANC_TILES // N_COL, N_COL, 1, 1)
    inner = jnp.arange(TILE, dtype=jnp.int32)
    same_cell = (inner[:, None] == inner[None, :]).reshape(1, 1, 1, 1, TILE, TILE)
    same = jnp.logical_and(row_tile == col_tile, same_cell)
    return noise * spread + jnp.where(same, 1.5, 0.0)


def block_levels(stream_key, shape, cuts, least, largest):
    gain = 1.0
    for position, shards_of in cuts:
        heights = jax.random.uniform(jax.random.fold_in(jax.random.fold_in(stream_key, 6), position), (shards_of,), jnp.float32, least / len(cuts), largest / len(cuts))
        gain = gain * jnp.repeat(jnp.exp(heights), shape[position] // shards_of).reshape((-1,) + (1,) * (len(shape) - 1 - position))
    return gain


def normal_values(own_key, dims, scale, reach, shards=(), kind=jnp.bfloat16):
    entries = jax.random.normal(own_key, dims, jnp.float32) * scale
    if len(shards) > 0:
        entries = block_levels(own_key, dims, shards, -0.22, 0.18) * entries
    return jnp.clip(entries, min=-reach, max=reach).astype(kind)


def setup_inputs(seed: int = 0) -> dict:
    seeds = jax.random.split(jax.random.key(seed), 9)
    return {
        "inverse": draw_inverse(jax.random.fold_in(seeds[8], 71), 0),
        "struct_first": draw_struct_first(jax.random.fold_in(seeds[8], 71), 0),
        "struct_second": draw_struct_second(jax.random.fold_in(seeds[8], 71), 0),
        "factor_first": normal_values(seeds[3], (LIST, TILE, TILE), 0.04, 0.25, ((0, 16),), jnp.float32),
        "factor_second": normal_values(seeds[4], (LIST2, TILE, TILE), 0.04, 0.25, ((0, 16),), jnp.float32),
        "link_factor": normal_values(seeds[5], (TILE, TILE), TILE ** -0.5, 0.375, (), jnp.float32),
        "dinv_first": normal_values(seeds[6], (TILE, TILE), 1.0, 6.0, (), jnp.float32),
        "dinv_second": normal_values(seeds[7], (TILE, TILE), 1.0, 6.0, (), jnp.float32),
    }


PRECISE = lax.Precision.HIGHEST


def column_panel(inverse_tiles, tile_ids, factor):
    def step_fn(totals, id_block):
        tile_id, factor_tile = id_block
        column = lax.dynamic_index_in_dim(inverse_tiles, tile_id, 1, keepdims=False)
        return totals + jnp.einsum('pxy,yz->pxz', column, factor_tile, precision=PRECISE), None

    start_sum = jnp.zeros((ANC_TILES, TILE, TILE), jnp.float32)
    result, _ = lax.scan(step_fn, start_sum, (tile_ids, factor))
    return result


def reference(inverse, struct_first, struct_second, factor_first, factor_second, link_factor, dinv_first, dinv_second):
    inverse_tiles = inverse.reshape(ANC_TILES, ANC_TILES, TILE, TILE)
    positions = jnp.arange(ANC_TILES, dtype=jnp.int32)
    owned_first = jnp.any(positions[:, None] == struct_first[None, :], axis=1)
    owned_second = jnp.any(positions[:, None] == struct_second[None, :], axis=1)
    panel_first = column_panel(inverse_tiles, struct_first, factor_first)
    column_first = jnp.where(owned_first[:, None, None], -panel_first, 0.0)
    diag_first = dinv_first + jnp.einsum('ixy,ixz->yz', factor_first, panel_first[struct_first], precision=PRECISE)
    panel_second = column_panel(inverse_tiles, struct_second, factor_second)
    panel_second = panel_second + jnp.einsum('pxy,yz->pxz', column_first, link_factor, precision=PRECISE)
    joined = jnp.einsum('jxy,jxz->yz', column_first[struct_second], factor_second, precision=PRECISE)
    joined = joined + jnp.dot(diag_first, link_factor, precision=PRECISE, preferred_element_type=jnp.float32)
    column_second = jnp.where(owned_second[:, None, None], -panel_second, 0.0)
    link_second = -joined
    diag_second = dinv_second + jnp.einsum('jxy,jxz->yz', factor_second, panel_second[struct_second], precision=PRECISE)
    diag_second = diag_second + jnp.dot(link_factor.T, joined, precision=PRECISE, preferred_element_type=jnp.float32)
    out_shape = (ANC_TILES // N_ROW, N_ROW, TILE, TILE)
    return (column_first.reshape(out_shape), diag_first, column_second.reshape(out_shape), link_second, diag_second)
```

```python
import functools

import jax
import jax.numpy as jnp
from jax import lax
from jax.experimental import pallas as pl
from jax.experimental.pallas import tpu as pltpu
from jax.sharding import PartitionSpec as P

MESH = pl.DeviceIdType.MESH
SIDE = 4
F32 = jnp.float32
BF16 = jnp.bfloat16


def split(v):
    hi = v.astype(BF16)
    return hi, (v - hi.astype(F32)).astype(BF16)


def mm(p, q):
    return jnp.dot(p, q, preferred_element_type=F32)


def dot3(p, q):
    ph, plo = split(p)
    qh, qlo = split(q)
    return mm(ph, qh) + (mm(ph, qlo) + mm(plo, qh))


def kernel(
    nr, nc, na, ns, f1, f2, width,
    tab, inv, fac1, fac2, link, dinv1, dinv2,
    o1, o2, o3,
    a_v, l_v, d1_v, d2_v, lt_v,
    pf, pg, pf2, pg2, st, cw, wh, wl, acc,
    hop, hopped, fb, ysum, zin, xb, frb, grb,
    st2, rb, m_v, rx, n_v, q_v, s_v, u_v, w_v,
    ld, lds, s1, pfr, pgr, pxs, pxr, bs, br, cs, cr,
    r1s, r1r, r2s, fbr, zs, zr, ts, tr, es, er, qs, qr, us, ur, vs, vr,
):
    r = lax.axis_index("row")
    c = lax.axis_index("col")
    k = lax.rem(r, 2)
    z = r // 2
    nz = nr // 2
    y = c // SIDE
    x = lax.rem(c, SIDE)
    mate = z * 2 + (1 - k)

    def remote(src, dst, ss, rs, row, col):
        return pltpu.make_async_remote_copy(
            src_ref=src, dst_ref=dst, send_sem=ss, recv_sem=rs,
            device_id=(row, col), device_id_type=MESH,
        )

    def take(ref, sem):
        pltpu.make_async_copy(ref, ref, sem).wait()

    def load_a(b):
        return pltpu.make_async_copy(inv.at[:, b], a_v.at[:, b], ld.at[b])

    small = [
        pltpu.make_async_copy(link, l_v, lds.at[0]),
        pltpu.make_async_copy(dinv1, d1_v, lds.at[1]),
        pltpu.make_async_copy(dinv2, d2_v, lds.at[2]),
    ]
    barrier = pltpu.get_barrier_semaphore()

    def greet_row(d, carry):
        pl.semaphore_signal(barrier, inc=1, device_id=(lax.rem(r + d, nr), c), device_id_type=MESH)
        return carry

    def greet_col(d, carry):
        pl.semaphore_signal(barrier, inc=1, device_id=(r, lax.rem(c + d, nc)), device_id_type=MESH)
        return carry

    lax.fori_loop(1, nr, greet_row, 0)
    lax.fori_loop(1, nc, greet_col, 0)
    row8 = pl.multiple_of(128 * k + 8 * c, 8)
    pltpu.make_async_copy(fac1.at[:, pl.ds(row8, 8), :], pf.at[pl.ds(r * f1, f1)], pfr).start()
    pltpu.make_async_copy(fac2.at[:, pl.ds(row8, 8), :], pg.at[pl.ds(r * f2, f2)], pgr).start()
    for cp in small:
        cp.start()
    for b in range(ns):
        load_a(b).start()
    pl.semaphore_wait(barrier, nr + nc - 2)

    def send_pieces(fac, buf, count, rsem):
        def go(d, carry):
            r2 = lax.rem(r + d, nr)
            k2 = lax.rem(r2, 2)
            rows = pl.multiple_of(128 * k2 + 8 * c, 8)
            remote(
                fac.at[:, pl.ds(rows, 8), :], buf.at[pl.ds(r * count, count)], s1, rsem, r2, c
            ).start()
            return carry

        lax.fori_loop(1, nr, go, 0)

    send_pieces(fac1, pf, f1, pfr)
    send_pieces(fac2, pg, f2, pgr)

    for cp in small:
        cp.wait()
    first = jnp.where(jnp.logical_and(r == 0, c == 0), 1.0, 0.0).astype(F32)
    lt_v[...] = jnp.transpose(l_v[...])
    d1_v[...] = jnp.transpose(d1_v[...]) * first
    d2_v[...] = jnp.transpose(d2_v[...]) * first

    take(pf, pfr)
    take(pg, pgr)
    swap_f = remote(pf, pf2, pxs.at[0], pxr.at[0], mate, c)
    swap_g = remote(pg, pg2, pxs.at[1], pxr.at[1], mate, c)

    def pack(b, carry):
        def one(c2, carry2):
            j1 = tab[0, b * nc + c2]
            j2 = tab[1, b * nc + c2]
            v1 = pf[jnp.maximum(j1, 0)]
            v2 = pg[jnp.maximum(j2, 0)]
            st[c2, b, 0] = jnp.where(j1 >= 0, v1, 0.0)
            st[c2, b, 1] = jnp.where(j2 >= 0, v2, 0.0)
            return carry2

        lax.fori_loop(0, nc, one, 0)
        pltpu.make_async_copy(st.at[c, b], cw.at[b, :, k, c], br.at[b]).start()

        def go(d, carry2):
            c2 = lax.rem(c + d, nc)
            remote(st.at[c2, b], cw.at[b, :, k, c], bs, br.at[b], r, c2).start()
            return carry2

        lax.fori_loop(1, nc, go, 0)
        return carry

    lax.fori_loop(0, ns, pack, 0)
    swap_f.start()
    swap_g.start()

    def ring(h):
        if h == 0:
            return x, y * SIDE + lax.rem(x + 1, SIDE), y * SIDE + lax.rem(x + SIDE - 1, SIDE)
        return y, lax.rem(y + 1, SIDE) * SIDE + x, lax.rem(y + SIDE - 1, SIDE) * SIDE + x

    half = SIDE // 2

    def part(a, h, who, lo, n):
        if h == 0:
            return acc.at[a, 0, pl.ds(lo, n), who]
        return acc.at[a, 1, who, pl.ds(lo, n)]

    def step_one(a):
        for h in range(2):
            u, right, left = ring(h)
            up, down, far = lax.rem(u + 1, SIDE), lax.rem(u + SIDE - 1, SIDE), lax.rem(u + 2, SIDE)
            remote(part(a, h, far, 0, half), hop.at[h, 0, a], r1s, r1r.at[h, 0, a], r, right).start()
            remote(part(a, h, far, half, half), hop.at[h, 1, a], r1s, r1r.at[h, 1, a], r, left).start()
            remote(
                part(a, h, up, half, half), fb.at[h, 0, a, pl.ds(half, half)], r1s, fbr.at[h, 0, a], r, right
            ).start()
            remote(
                part(a, h, down, 0, half), fb.at[h, 1, a, pl.ds(0, half)], r1s, fbr.at[h, 1, a], r, left
            ).start()

    def exchange(b):
        return remote(cw.at[b, :, k], cw.at[b, :, k], cs, cr.at[b], mate, c)

    def slot(b):
        ff = cw[b, 0].reshape(256, 256)
        gg = cw[b, 1].reshape(256, 256)
        hh = gg - dot3(ff, l_v[...])
        fh, fl = split(ff)
        hhi, hlo = split(hh)
        wh[:, 0:256] = fh
        wl[:, 0:256] = fl
        wh[:, 256:512] = hhi
        wl[:, 256:512] = hlo
        load_a(b).wait()

        def rowstep(a, carry):
            ah, al = split(a_v[a, b])
            got = mm(ah, wh[...]) + (mm(ah, wl[...]) + mm(al, wh[...]))
            got = got.reshape(2, SIDE, SIDE, 8, 512)

            @pl.when(b == 0)
            def _():
                acc[a] = got

            @pl.when(b > 0)
            def _():
                acc[a] += got

            @pl.when(b == ns - 1)
            def _():
                step_one(a)

            return carry

        lax.fori_loop(0, na, rowstep, 0)

    def slots(b, carry):
        @pl.when(b < ns)
        def _():
            take(cw.at[b, :, k], br.at[b])
            exchange(b).start()

        @pl.when(b > 0)
        def _():
            take(cw.at[b - 1, :, k], cr.at[b - 1])
            slot(b - 1)

        return carry

    lax.fori_loop(0, ns + 1, slots, 0)

    def step_two(a, carry):
        for h in range(2):
            u, right, left = ring(h)
            up, down = lax.rem(u + 1, SIDE), lax.rem(u + SIDE - 1, SIDE)
            take(hop.at[h, 0, a], r1r.at[h, 0, a])
            hopped[h, 0, a] = hop[h, 0, a] + part(a, h, up, 0, half)[...]
            remote(
                hopped.at[h, 0, a], fb.at[h, 0, a, pl.ds(0, half)], r2s, fbr.at[h, 0, a], r, right
            ).start()
            take(hop.at[h, 1, a], r1r.at[h, 1, a])
            hopped[h, 1, a] = hop[h, 1, a] + part(a, h, down, half, half)[...]
            remote(
                hopped.at[h, 1, a], fb.at[h, 1, a, pl.ds(half, half)], r2s, fbr.at[h, 1, a], r, left
            ).start()
        return carry

    lax.fori_loop(0, na, step_two, 0)

    swap_f.wait()
    swap_g.wait()
    frb[...] = jnp.zeros_like(frb)
    grb[...] = jnp.zeros_like(grb)
    xb[...] = jnp.zeros_like(xb)
    for a in range(na):
        j1 = tab[0, a * nr + r]
        j2 = tab[1, a * nr + r]
        for h in range(2):
            lo = a * 16 + h * 8
            i1, i2 = jnp.maximum(j1, 0), jnp.maximum(j2, 0)
            frb[lo:lo + 8, :] = jnp.where(j1 >= 0, jnp.where(k == h, pf[i1], pf2[i1]), 0.0)
            grb[lo:lo + 8, :] = jnp.where(j2 >= 0, jnp.where(k == h, pg[i2], pg2[i2]), 0.0)

    def second(a, carry):
        for h in range(2):
            u = ring(h)[0]
            take(fb.at[h, 0, a], fbr.at[h, 0, a])
            take(fb.at[h, 1, a], fbr.at[h, 1, a])
            ysum[h, a] = part(a, h, u, 0, SIDE)[...] + (fb[h, 0, a] + fb[h, 1, a])
            v = y if h == 0 else x
            for d in range(1, SIDE):
                v2 = lax.rem(v + d, SIDE)
                col = v2 * SIDE + x if h == 0 else y * SIDE + v2
                remote(ysum.at[h, a, v2], zin.at[h, a, d - 1], zs, zr.at[h, a], r, col).start()
        return carry

    lax.fori_loop(0, na, second, 0)

    def gather(a, carry):
        for h in range(2):
            v = y if h == 0 else x
            take(zin.at[h, a], zr.at[h, a])
            tot = ysum[h, a, v] + (zin[h, a, 0] + zin[h, a, 1] + zin[h, a, 2])
            xb[pl.ds(pl.multiple_of(a * 16 + h * 8, 8), 8), :] = tot
        return carry

    lax.fori_loop(0, na, gather, 0)

    lane = lax.broadcasted_iota(jnp.int32, (16, 128), 1) // 16
    for c2 in range(nc):
        blk, off = c2 // 8, c2 % 8
        for q in range(width // 128):
            val = jnp.zeros((16, 128), F32)
            for g in range(8):
                p = q * 8 + g
                if p < 2 * na:
                    fg, a = p // na, p % na
                    src = xb[a * 16:a * 16 + 16, fg * 256 + blk * 128:fg * 256 + blk * 128 + 128]
                    shift = (16 * (g - off)) % 128
                    if shift:
                        src = pltpu.roll(src, shift, axis=1)
                    val = jnp.where(lane == g, src, val)
            st2[c2, :, :, q * 128:(q + 1) * 128] = val.reshape(2, 8, 128)
    pltpu.make_async_copy(st2.at[c], rb.at[:, c], tr).start()

    def send_cols(d, carry):
        c2 = lax.rem(c + d, nc)
        remote(st2.at[c2], rb.at[:, c], ts, tr, r, c2).start()
        return carry

    lax.fori_loop(1, nc, send_cols, 0)

    x1 = xb[:, 0:256]
    x2 = xb[:, 256:512]
    d1t = dot3(jnp.transpose(x1), frb[...]) + d1_v[...]
    m_v[0] = d1t.reshape(nc, 2, 8, 256)
    jt = dot3(lt_v[...], d1t) - dot3(jnp.transpose(grb[...]), x1)
    m_v[1] = jt.reshape(nc, 2, 8, 256)
    et = dot3(jnp.transpose(x2), grb[...]) + dot3(jt, l_v[...]) + d2_v[...]
    m_v[2] = et.reshape(nc, 2, 8, 256)
    fold = remote(m_v.at[:, :, 1 - k], rx, es, er, mate, c)
    fold.start()
    take(rx, er)
    for t in range(3):
        n_v[t] = m_v[t, :, k] + rx[t]
    pltpu.make_async_copy(n_v.at[:, c], q_v.at[c], qr).start()

    def send_terms(d, carry):
        c2 = lax.rem(c + d, nc)
        remote(n_v.at[:, c2], q_v.at[c], qs, qr, r, c2).start()
        return carry

    lax.fori_loop(1, nc, send_terms, 0)

    take(rb, tr)
    cols = jnp.transpose(rb[...].reshape(256, width))
    for a in range(na):
        j1 = tab[0, a * nr + r]
        j2 = tab[1, a * nr + r]
        o1[a * 16:(a + 1) * 16, :] = jnp.where(j1 >= 0, -cols[a * 16:(a + 1) * 16, :], 0.0)
        lo = (na + a) * 16
        o2[a * 16:(a + 1) * 16, :] = jnp.where(j2 >= 0, -cols[lo:lo + 16, :], 0.0)

    take(q_v, qr)
    tot = q_v[0]
    for i in range(1, nc):
        tot = tot + q_v[i]
    s_v[...] = tot
    pltpu.make_async_copy(s_v, u_v.at[z], ur).start()

    def send_z(d, carry):
        z2 = lax.rem(z + d, nz)
        remote(s_v, u_v.at[z], us, ur, z2 * 2 + k, c).start()
        return carry

    if nz > 1:
        lax.fori_loop(1, nz, send_z, 0)
    take(u_v, ur)
    tot = u_v[0]
    for i in range(1, nz):
        tot = tot + u_v[i]
    w_v[k] = tot
    last = remote(w_v.at[k], w_v.at[k], vs, vr, mate, c)
    last.start()
    take(w_v.at[k], vr)
    for h in range(2):
        o3[0, h * 8:(h + 1) * 8] = w_v[h, 0]
        o3[1, h * 8:(h + 1) * 8] = -w_v[h, 1]
        o3[2, h * 8:(h + 1) * 8] = w_v[h, 2]

    take(pf.at[pl.ds(0, (nr - 1) * f1)], s1)
    take(pg.at[pl.ds(0, (nr - 1) * f2)], s1)
    take(st.at[pl.ds(0, nc - 1)], bs)
    take(cw.at[:, :, 0], cs)
    take(fb, r1s)
    take(hop, r2s)
    take(zin, zs)
    take(rb.at[:, pl.ds(0, nc - 1)], ts)
    take(rx, es)
    take(q_v.at[pl.ds(0, nc - 1)], qs)
    if nz > 1:
        take(u_v.at[pl.ds(0, nz - 1)], us)
    take(w_v.at[0], vs)


def body(inverse, struct_first, struct_second, factor_first, factor_second, link_factor, dinv_first, dinv_second):
    nr = lax.axis_size("row")
    nc = lax.axis_size("col")
    na, _, ns, _, ext, _ = inverse.shape
    f1, f2 = factor_first.shape[0], factor_second.shape[0]
    tiles = max(na * nr, ns * nc)
    ids = jnp.arange(tiles, dtype=jnp.int32)

    def where_is(ids_of):
        n = ids_of.shape[0]
        spot = jnp.arange(1, n + 1, dtype=jnp.int32)
        return jnp.sum(jnp.where(ids[:, None] == ids_of[None, :], spot[None, :], 0), axis=1) - 1

    tab = jnp.stack([where_is(struct_first), where_is(struct_second)])
    width = -(-2 * na * 16 // 128) * 128
    deep = -(-na * 16 // 128) * 128
    any_spec = pl.BlockSpec(memory_space=pl.ANY)
    vm = lambda *s: pltpu.VMEM(s, F32)
    dma = pltpu.SemaphoreType.DMA
    half = SIDE // 2
    o1, o2, o3 = pl.pallas_call(
        functools.partial(kernel, nr, nc, na, ns, f1, f2, width),
        out_shape=(
            jax.ShapeDtypeStruct((na * 16, 256), F32),
            jax.ShapeDtypeStruct((na * 16, 256), F32),
            jax.ShapeDtypeStruct((3, 16, 256), F32),
        ),
        in_specs=[pl.BlockSpec(memory_space=pltpu.SMEM)] + [any_spec] * 6,
        out_specs=(pl.BlockSpec(memory_space=pltpu.VMEM),) * 3,
        scratch_shapes=[
            vm(na, ns, 256, 256), vm(256, 256), vm(256, 256), vm(256, 256), vm(256, 256),
            vm(nr * f1, 8, 256), vm(nr * f2, 8, 256), vm(nr * f1, 8, 256), vm(nr * f2, 8, 256),
            vm(nc, ns, 2, 8, 256), vm(ns, 2, 2, nc, 8, 256),
            pltpu.VMEM((256, 512), BF16), pltpu.VMEM((256, 512), BF16),
            vm(na, 2, SIDE, SIDE, 8, 512),
            vm(2, 2, na, half, 8, 512), vm(2, 2, na, half, 8, 512),
            vm(2, 2, na, SIDE, 8, 512), vm(2, na, SIDE, 8, 512),
            vm(2, na, SIDE - 1, 8, 512),
            vm(deep, 512), vm(deep, 256), vm(deep, 256),
            vm(nc, 2, 8, width), vm(2, nc, 8, width),
            vm(3, nc, 2, 8, 256), vm(3, nc, 8, 256), vm(3, nc, 8, 256), vm(nc, 3, 8, 256),
            vm(3, 8, 256), vm(nr // 2, 3, 8, 256), vm(2, 3, 8, 256),
            dma((ns,)), dma((3,)), dma, dma, dma, dma((2,)), dma((2,)), dma, dma((ns,)), dma, dma((ns,)),
            dma, dma((2, 2, na)), dma, dma((2, 2, na)), dma, dma((2, na)),
            dma, dma, dma, dma, dma, dma, dma, dma, dma, dma,
        ],
        compiler_params=pltpu.CompilerParams(
            collective_id=0, has_side_effects=True, vmem_limit_bytes=56 * 1024 * 1024
        ),
    )(tab, inverse.reshape(na, ns, ext, ext), factor_first, factor_second, link_factor, dinv_first, dinv_second)
    panel = lambda o: jnp.swapaxes(o.reshape(na, 1, 16, 256), 2, 3)
    turn = jnp.swapaxes
    return (panel(o1), turn(o3[0], 0, 1), panel(o2), turn(o3[1], 0, 1), turn(o3[2], 0, 1))


def solution(mesh):
    placed = (
        P(None, "row", None, "col", None, None),
        P(),
        P(),
        P("row", None, None),
        P("row", None, None),
        P(),
        P(),
        P(),
    )
    return jax.shard_map(
        body,
        mesh=mesh,
        in_specs=placed,
        out_specs=(
            P(None, "row", None, "col"),
            P(None, "col"),
            P(None, "row", None, "col"),
            P(None, "col"),
            P(None, "col"),
        ),
        check_vma=False,
    )
```

```python
import functools

import jax
import jax.numpy as jnp
from jax import lax
from jax.experimental import pallas as pl
from jax.experimental.pallas import tpu as pltpu
from jax.sharding import PartitionSpec as P

MESH = pl.DeviceIdType.MESH
SIDE = 4
F32 = jnp.float32
BF16 = jnp.bfloat16


def split(v):
    hi = v.astype(BF16)
    return hi, (v - hi.astype(F32)).astype(BF16)


def mm(p, q):
    return jnp.dot(p, q, preferred_element_type=F32)


def dot3(p, q):
    ph, plo = split(p)
    qh, qlo = split(q)
    return mm(ph, qh) + (mm(ph, qlo) + mm(plo, qh))


def kernel(
    nr, nc, na, ns, f1, f2, width,
    ids1, ids2, inv, fac1, fac2, link, dinv1, dinv2,
    out,
    tab_v, tab, a_v, l_v, d1_v, d2_v, lt_v,
    pf, pg, rps, rp, st, cw, wh, wl, acc,
    hop, hopped, fb, ysum, zin, xb, frb, grb,
    st2, rb, m_v, rx, n_v, q_v, s_v, u_v, w_v,
    ld, lds, lt, s1, pfr, pgr, rs_, rr, bs, br, zxs, zxr, cs, cr,
    r1s, r1r, r2s, fbr, zs, zr, ts, tr, es, er, qs, qr, us, ur, vs, vr,
):
    r = lax.axis_index("row")
    c = lax.axis_index("col")
    k = lax.rem(r, 2)
    z = r // 2
    nz = nr // 2
    y = c // SIDE
    x = lax.rem(c, SIDE)
    e = lax.rem(z, 2)
    mate = z * 2 + (1 - k)
    z_up = lax.rem(z + 1, nz) * 2 + k
    z_down = lax.rem(z + nz - 1, nz) * 2 + k
    lanes = pl.multiple_of(128 * e, 128)

    def remote(src, dst, ss, rs, row, col):
        return pltpu.make_async_remote_copy(
            src_ref=src, dst_ref=dst, send_sem=ss, recv_sem=rs,
            device_id=(row, col), device_id_type=MESH,
        )

    def take(ref, sem):
        pltpu.make_async_copy(ref, ref, sem).wait()

    def load_a(b):
        return pltpu.make_async_copy(inv.at[:, b], a_v.at[:, b], ld.at[b])

    small = [
        pltpu.make_async_copy(link, l_v, lds.at[0]),
        pltpu.make_async_copy(dinv1, d1_v, lds.at[1]),
        pltpu.make_async_copy(dinv2, d2_v, lds.at[2]),
    ]
    barrier = pltpu.get_barrier_semaphore()

    def greet_row(d, carry):
        pl.semaphore_signal(barrier, inc=1, device_id=(lax.rem(r + d, nr), c), device_id_type=MESH)
        return carry

    def greet_col(d, carry):
        pl.semaphore_signal(barrier, inc=1, device_id=(r, lax.rem(c + d, nc)), device_id_type=MESH)
        return carry

    lax.fori_loop(1, nr, greet_row, 0)
    lax.fori_loop(1, nc, greet_col, 0)
    row8 = pl.multiple_of(128 * k + 8 * c, 8)
    pltpu.make_async_copy(fac1.at[:, pl.ds(row8, 8), pl.ds(lanes, 128)], pf.at[pl.ds(r * f1, f1)], pfr).start()
    pltpu.make_async_copy(fac2.at[:, pl.ds(row8, 8), pl.ds(lanes, 128)], pg.at[pl.ds(r * f2, f2)], pgr).start()
    for cp in small:
        cp.start()
    for b in range(ns):
        load_a(b).start()
    tile = lax.broadcasted_iota(jnp.int32, (8, 128), 1)
    which = lax.broadcasted_iota(jnp.int32, (8, 128), 0)
    spot = jnp.full((8, 128), -1, jnp.int32)
    for t, ids in ((0, ids1), (1, ids2)):
        for j in range(ids.shape[0]):
            spot = jnp.where(jnp.logical_and(tile == ids[j], which == t), j, spot)
    tab_v[...] = spot
    to_smem = pltpu.make_async_copy(tab_v, tab, lt)
    to_smem.start()
    for cp in small:
        cp.wait()
    first = jnp.where(jnp.logical_and(r == 0, c == 0), 1.0, 0.0).astype(F32)
    lt_v[...] = jnp.transpose(l_v[...])
    d1_v[...] = jnp.transpose(d1_v[...]) * first
    d2_v[...] = jnp.transpose(d2_v[...]) * first

    to_smem.wait()
    pl.semaphore_wait(barrier, nr + nc - 2)

    def send_pieces(fac, buf, count, rsem):
        def go(d, carry):
            r2 = lax.rem(r + d, nr)
            k2 = lax.rem(r2, 2)
            rows = pl.multiple_of(128 * k2 + 8 * c, 8)
            side = pl.multiple_of(128 * lax.rem(r2 // 2, 2), 128)
            remote(
                fac.at[:, pl.ds(rows, 8), pl.ds(side, 128)], buf.at[pl.ds(r * count, count)], s1, rsem, r2, c
            ).start()
            return carry

        lax.fori_loop(1, nr, go, 0)

    send_pieces(fac1, pf, f1, pfr)
    send_pieces(fac2, pg, f2, pgr)

    take(pf, pfr)
    take(pg, pgr)

    def pack(b, carry):
        def one(c2, carry2):
            j1 = tab[0, b * nc + c2]
            j2 = tab[1, b * nc + c2]
            v1 = pf[jnp.maximum(j1, 0)]
            v2 = pg[jnp.maximum(j2, 0)]
            st[c2, b, 0] = jnp.where(j1 >= 0, v1, 0.0)
            st[c2, b, 1] = jnp.where(j2 >= 0, v2, 0.0)
            return carry2

        lax.fori_loop(0, nc, one, 0)
        pltpu.make_async_copy(st.at[c, b], cw.at[b, :, e, k, c], br.at[b]).start()

        def go(d, carry2):
            c2 = lax.rem(c + d, nc)
            remote(st.at[c2, b], cw.at[b, :, e, k, c], bs, br.at[b], r, c2).start()
            return carry2

        lax.fori_loop(1, nc, go, 0)
        return carry

    lax.fori_loop(0, ns, pack, 0)

    other = z + 1 - 2 * e
    for t in range(4):
        z2 = z if t < 2 else other
        k2 = k if t % 2 == 0 else 1 - k
        r2 = z2 * 2 + k2
        for a in range(na):
            j1 = tab[0, a * nr + r2]
            j2 = tab[1, a * nr + r2]
            rps[t, 0, a] = jnp.where(j1 >= 0, pf[jnp.maximum(j1, 0)], 0.0)
            rps[t, 1, a] = jnp.where(j2 >= 0, pg[jnp.maximum(j2, 0)], 0.0)
        if t == 0:
            pltpu.make_async_copy(rps.at[t], rp.at[e * 2 + k], rr).start()
        else:
            remote(rps.at[t], rp.at[e * 2 + k], rs_, rr, r2, c).start()

    def ring(h):
        if h == 0:
            return x, y * SIDE + lax.rem(x + 1, SIDE), y * SIDE + lax.rem(x + SIDE - 1, SIDE)
        return y, lax.rem(y + 1, SIDE) * SIDE + x, lax.rem(y + SIDE - 1, SIDE) * SIDE + x

    half = SIDE // 2

    def part(a, h, who, lo, n):
        if h == 0:
            return acc.at[a, 0, pl.ds(lo, n), who]
        return acc.at[a, 1, who, pl.ds(lo, n)]

    def step_one(a):
        for h in range(2):
            u, right, left = ring(h)
            up, down, far = lax.rem(u + 1, SIDE), lax.rem(u + SIDE - 1, SIDE), lax.rem(u + 2, SIDE)
            remote(part(a, h, far, 0, half), hop.at[h, 0, a], r1s, r1r.at[h, 0, a], r, right).start()
            remote(part(a, h, far, half, half), hop.at[h, 1, a], r1s, r1r.at[h, 1, a], r, left).start()
            remote(
                part(a, h, up, half, half), fb.at[h, 0, a, pl.ds(half, half)], r1s, fbr.at[h, 0, a], r, right
            ).start()
            remote(
                part(a, h, down, 0, half), fb.at[h, 1, a, pl.ds(0, half)], r1s, fbr.at[h, 1, a], r, left
            ).start()

    def slot(b):
        ff = jnp.concatenate([cw[b, 0, 0].reshape(256, 128), cw[b, 0, 1].reshape(256, 128)], axis=1)
        gg = jnp.concatenate([cw[b, 1, 0].reshape(256, 128), cw[b, 1, 1].reshape(256, 128)], axis=1)
        hh = gg - dot3(ff, l_v[...])
        fh, fl = split(ff)
        hhi, hlo = split(hh)
        wh[:, 0:256] = fh
        wl[:, 0:256] = fl
        wh[:, 256:512] = hhi
        wl[:, 256:512] = hlo
        load_a(b).wait()

        def rowstep(a, carry):
            ah, al = split(a_v[a, b])
            got = mm(ah, wh[...]) + (mm(ah, wl[...]) + mm(al, wh[...]))
            got = got.reshape(2, SIDE, SIDE, 8, 512)

            @pl.when(b == 0)
            def _():
                acc[a] = got

            @pl.when(b > 0)
            def _():
                acc[a] += got

            @pl.when(b == ns - 1)
            def _():
                step_one(a)

            return carry

        lax.fori_loop(0, na, rowstep, 0)

    def slots(b, carry):
        @pl.when(b < ns)
        def _():
            mine = cw.at[b, :, e, k]
            take(mine, br.at[b])
            remote(mine, mine, cs, cr.at[b], mate, c).start()
            remote(cw.at[b, 0, e, k], cw.at[b, 0, e, k], zxs, zxr.at[b], z_down, c).start()
            remote(cw.at[b, 1, e, k], cw.at[b, 1, e, k], zxs, zxr.at[b], z_up, c).start()

        @pl.when(jnp.logical_and(b > 0, b <= ns))
        def _():
            got = cw.at[b - 1, :, 1 - e, k]
            take(got, zxr.at[b - 1])
            remote(got, got, cs, cr.at[b - 1], mate, c).start()

        @pl.when(b > 1)
        def _():
            take(cw.at[b - 2, :, :, 1 - k], cr.at[b - 2])
            slot(b - 2)

        return carry

    lax.fori_loop(0, ns + 2, slots, 0)

    def step_two(a, carry):
        for h in range(2):
            u, right, left = ring(h)
            up, down = lax.rem(u + 1, SIDE), lax.rem(u + SIDE - 1, SIDE)
            take(hop.at[h, 0, a], r1r.at[h, 0, a])
            hopped[h, 0, a] = hop[h, 0, a] + part(a, h, up, 0, half)[...]
            remote(
                hopped.at[h, 0, a], fb.at[h, 0, a, pl.ds(0, half)], r2s, fbr.at[h, 0, a], r, right
            ).start()
            take(hop.at[h, 1, a], r1r.at[h, 1, a])
            hopped[h, 1, a] = hop[h, 1, a] + part(a, h, down, half, half)[...]
            remote(
                hopped.at[h, 1, a], fb.at[h, 1, a, pl.ds(half, half)], r2s, fbr.at[h, 1, a], r, left
            ).start()
        return carry

    lax.fori_loop(0, na, step_two, 0)

    take(rp, rr)
    frb[...] = jnp.zeros_like(frb)
    grb[...] = jnp.zeros_like(grb)
    xb[...] = jnp.zeros_like(xb)
    for a in range(na):
        for h in range(2):
            lo = a * 16 + h * 8
            for g in range(2):
                frb[lo:lo + 8, g * 128:g * 128 + 128] = rp[g * 2 + h, 0, a]
                grb[lo:lo + 8, g * 128:g * 128 + 128] = rp[g * 2 + h, 1, a]

    def second(a, carry):
        for h in range(2):
            u = ring(h)[0]
            take(fb.at[h, 0, a], fbr.at[h, 0, a])
            take(fb.at[h, 1, a], fbr.at[h, 1, a])
            ysum[h, a] = part(a, h, u, 0, SIDE)[...] + (fb[h, 0, a] + fb[h, 1, a])
            v = y if h == 0 else x
            for d in range(1, SIDE):
                v2 = lax.rem(v + d, SIDE)
                col = v2 * SIDE + x if h == 0 else y * SIDE + v2
                remote(ysum.at[h, a, v2], zin.at[h, a, d - 1], zs, zr.at[h, a], r, col).start()
        return carry

    lax.fori_loop(0, na, second, 0)

    def gather(a, carry):
        for h in range(2):
            v = y if h == 0 else x
            take(zin.at[h, a], zr.at[h, a])
            tot = ysum[h, a, v] + (zin[h, a, 0] + zin[h, a, 1] + zin[h, a, 2])
            xb[pl.ds(pl.multiple_of(a * 16 + h * 8, 8), 8), :] = tot
        return carry

    lax.fori_loop(0, na, gather, 0)

    x1 = xb[:, 0:256]
    x2 = xb[:, 256:512]
    d1t = dot3(jnp.transpose(x1), frb[...]) + d1_v[...]
    m_v[0] = d1t.reshape(nc, 2, 8, 256)
    jt = dot3(lt_v[...], d1t) - dot3(jnp.transpose(grb[...]), x1)
    m_v[1] = jt.reshape(nc, 2, 8, 256)
    et = dot3(jnp.transpose(x2), grb[...]) + dot3(jt, l_v[...]) + d2_v[...]
    m_v[2] = et.reshape(nc, 2, 8, 256)
    fold = remote(m_v.at[:, :, 1 - k], rx, es, er, mate, c)
    fold.start()

    lane = lax.broadcasted_iota(jnp.int32, (16, 128), 1) // 16
    for c2 in range(nc):
        blk, off = c2 // 8, c2 % 8
        for q in range(width // 128):
            val = jnp.zeros((16, 128), F32)
            for g in range(8):
                p = q * 8 + g
                if p < 2 * na:
                    fg, a = p // na, p % na
                    src = xb[a * 16:a * 16 + 16, fg * 256 + blk * 128:fg * 256 + blk * 128 + 128]
                    shift = (16 * (g - off)) % 128
                    if shift:
                        src = pltpu.roll(src, shift, axis=1)
                    val = jnp.where(lane == g, src, val)
            st2[c2, :, :, q * 128:(q + 1) * 128] = val.reshape(2, 8, 128)

    take(rx, er)
    for t in range(3):
        n_v[t] = m_v[t, :, k] + rx[t]
    pltpu.make_async_copy(n_v.at[:, c], q_v.at[c], qr).start()

    def send_terms(d, carry):
        c2 = lax.rem(c + d, nc)
        remote(n_v.at[:, c2], q_v.at[c], qs, qr, r, c2).start()
        return carry

    lax.fori_loop(1, nc, send_terms, 0)

    pltpu.make_async_copy(st2.at[c], rb.at[:, c], tr).start()

    def send_cols(d, carry):
        c2 = lax.rem(c + d, nc)
        remote(st2.at[c2], rb.at[:, c], ts, tr, r, c2).start()
        return carry

    lax.fori_loop(1, nc, send_cols, 0)

    take(rb, tr)
    cols = jnp.transpose(rb[...].reshape(256, width))
    for a in range(na):
        j1 = tab[0, a * nr + r]
        j2 = tab[1, a * nr + r]
        out[a * 16:(a + 1) * 16, :] = jnp.where(j1 >= 0, -cols[a * 16:(a + 1) * 16, :], 0.0)
        lo = (na + a) * 16
        out[lo:lo + 16, :] = jnp.where(j2 >= 0, -cols[lo:lo + 16, :], 0.0)

    take(q_v, qr)
    tot = q_v[0]
    for i in range(1, nc):
        tot = tot + q_v[i]
    s_v[...] = tot
    pltpu.make_async_copy(s_v, u_v.at[z], ur).start()

    def send_z(d, carry):
        z2 = lax.rem(z + d, nz)
        remote(s_v, u_v.at[z], us, ur, z2 * 2 + k, c).start()
        return carry

    if nz > 1:
        lax.fori_loop(1, nz, send_z, 0)
    take(u_v, ur)
    tot = u_v[0]
    for i in range(1, nz):
        tot = tot + u_v[i]
    w_v[k] = tot
    last = remote(w_v.at[k], w_v.at[k], vs, vr, mate, c)
    last.start()
    take(w_v.at[k], vr)
    for h in range(2):
        lo = na * 32 + h * 8
        out[lo:lo + 8, :] = w_v[h, 0]
        out[lo + 16:lo + 24, :] = -w_v[h, 1]
        out[lo + 32:lo + 40, :] = w_v[h, 2]

    take(pf.at[pl.ds(0, (nr - 1) * f1)], s1)
    take(pg.at[pl.ds(0, (nr - 1) * f2)], s1)
    take(st.at[pl.ds(0, nc - 1)], bs)
    take(cw.at[:, :, :, 0], cs)
    take(cw.at[:, :, 0, 0], zxs)
    take(rp.at[pl.ds(0, 3)], rs_)
    take(fb, r1s)
    take(hop, r2s)
    take(zin, zs)
    take(rb.at[:, pl.ds(0, nc - 1)], ts)
    take(rx, es)
    take(q_v.at[pl.ds(0, nc - 1)], qs)
    if nz > 1:
        take(u_v.at[pl.ds(0, nz - 1)], us)
    take(w_v.at[0], vs)


def body(inverse, struct_first, struct_second, factor_first, factor_second, link_factor, dinv_first, dinv_second):
    nr = lax.axis_size("row")
    nc = lax.axis_size("col")
    na, _, ns, _, ext, _ = inverse.shape
    f1, f2 = factor_first.shape[0], factor_second.shape[0]
    width = -(-2 * na * 16 // 128) * 128
    deep = -(-na * 16 // 128) * 128
    any_spec = pl.BlockSpec(memory_space=pl.ANY)
    vm = lambda *s: pltpu.VMEM(s, F32)
    dma = pltpu.SemaphoreType.DMA
    half = SIDE // 2
    rows = na * 16
    o = pl.pallas_call(
        functools.partial(kernel, nr, nc, na, ns, f1, f2, width),
        out_shape=jax.ShapeDtypeStruct((2 * rows + 48, 256), F32),
        in_specs=[pl.BlockSpec(memory_space=pltpu.SMEM)] * 2 + [any_spec] * 6,
        out_specs=pl.BlockSpec(memory_space=pltpu.VMEM),
        scratch_shapes=[
            pltpu.VMEM((8, 128), jnp.int32), pltpu.SMEM((8, 128), jnp.int32),
            vm(na, ns, 256, 256), vm(256, 256), vm(256, 256), vm(256, 256), vm(256, 256),
            vm(nr * f1, 8, 128), vm(nr * f2, 8, 128), vm(4, 2, na, 8, 128), vm(4, 2, na, 8, 128),
            vm(nc, ns, 2, 8, 128), vm(ns, 2, 2, 2, nc, 8, 128),
            pltpu.VMEM((256, 512), BF16), pltpu.VMEM((256, 512), BF16),
            vm(na, 2, SIDE, SIDE, 8, 512),
            vm(2, 2, na, half, 8, 512), vm(2, 2, na, half, 8, 512),
            vm(2, 2, na, SIDE, 8, 512), vm(2, na, SIDE, 8, 512),
            vm(2, na, SIDE - 1, 8, 512),
            vm(deep, 512), vm(deep, 256), vm(deep, 256),
            vm(nc, 2, 8, width), vm(2, nc, 8, width),
            vm(3, nc, 2, 8, 256), vm(3, nc, 8, 256), vm(3, nc, 8, 256), vm(nc, 3, 8, 256),
            vm(3, 8, 256), vm(nr // 2, 3, 8, 256), vm(2, 3, 8, 256),
            dma((ns,)), dma((3,)), dma, dma, dma, dma, dma, dma, dma, dma((ns,)), dma, dma((ns,)), dma, dma((ns,)),
            dma, dma((2, 2, na)), dma, dma((2, 2, na)), dma, dma((2, na)),
            dma, dma, dma, dma, dma, dma, dma, dma, dma, dma,
        ],
        compiler_params=pltpu.CompilerParams(
            collective_id=0, has_side_effects=True, vmem_limit_bytes=56 * 1024 * 1024
        ),
    )(struct_first, struct_second, inverse.reshape(na, ns, ext, ext), factor_first, factor_second, link_factor, dinv_first, dinv_second)
    panel = lambda v: jnp.swapaxes(v.reshape(na, 1, 16, 256), 2, 3)
    turn = lambda n: jnp.swapaxes(o[2 * rows + 16 * n:2 * rows + 16 * n + 16], 0, 1)
    return (panel(o[:rows]), turn(0), panel(o[rows:2 * rows]), turn(1), turn(2))


def solution(mesh):
    placed = (
        P(None, "row", None, "col", None, None),
        P(),
        P(),
        P("row", None, None),
        P("row", None, None),
        P(),
        P(),
        P(),
    )
    return jax.shard_map(
        body,
        mesh=mesh,
        in_specs=placed,
        out_specs=(
            P(None, "row", None, "col"),
            P(None, "col"),
            P(None, "row", None, "col"),
            P(None, "col"),
            P(None, "col"),
        ),
        check_vma=False,
    )
```

```python
import functools

import jax
import jax.numpy as jnp
from jax import lax
from jax.experimental import pallas as pl
from jax.experimental.pallas import tpu as pltpu
from jax.sharding import PartitionSpec as P

MESH = pl.DeviceIdType.MESH
SIDE = 4
F32 = jnp.float32
BF16 = jnp.bfloat16


def split(v):
    hi = v.astype(BF16)
    return hi, (v - hi.astype(F32)).astype(BF16)


def mm(p, q):
    return jnp.dot(p, q, preferred_element_type=F32)


def dot3(p, q):
    ph, plo = split(p)
    qh, qlo = split(q)
    return mm(ph, qh) + (mm(ph, qlo) + mm(plo, qh))


def kernel(
    nr, nc, na, ns, f1, f2, n1, n2, width,
    ids1, ids2, inv, fac1, fac2, link, dinv1, dinv2,
    out,
    tab_v, tab, a_v, l_v, d1_v, d2_v, lt_v,
    pf, pg, rps, rp, st, cw1, cw2, w3, acc,
    hop, hopped, fb, ysum, zin, x1b, x2b, frb, grb,
    st2, rb, m_v, rx, n_v, q_v, s_v, u_v, w_v,
    ld, lds, lt, s1, pfr, pgr, rs_, rr, bs, br, zxs, zxr, cs, cr,
    r1s, r1r, r2s, fbr, zs, zr, ts, tr, es, er, qs, qr, us, ur, vs, vr,
):
    r = lax.axis_index("row")
    c = lax.axis_index("col")
    k = lax.rem(r, 2)
    z = r // 2
    nz = nr // 2
    y = c // SIDE
    x = lax.rem(c, SIDE)
    e = lax.rem(z, 2)
    mate = z * 2 + (1 - k)
    z_up = lax.rem(z + 1, nz) * 2 + k
    z_down = lax.rem(z + nz - 1, nz) * 2 + k
    lanes = pl.multiple_of(128 * e, 128)
    nu = n1 + n2
    row1, row2, rowi, rowp, rowq = 0, 8, 16, 24, 25

    def remote(src, dst, ss, rs, row, col):
        return pltpu.make_async_remote_copy(
            src_ref=src, dst_ref=dst, send_sem=ss, recv_sem=rs,
            device_id=(row, col), device_id_type=MESH,
        )

    def take(ref, sem):
        pltpu.make_async_copy(ref, ref, sem).wait()

    def load_a(b):
        return pltpu.make_async_copy(inv.at[:, b], a_v.at[:, b], ld.at[b])

    small = [
        pltpu.make_async_copy(link, l_v, lds.at[0]),
        pltpu.make_async_copy(dinv1, d1_v, lds.at[1]),
        pltpu.make_async_copy(dinv2, d2_v, lds.at[2]),
    ]
    barrier = pltpu.get_barrier_semaphore()

    def greet_row(d, carry):
        pl.semaphore_signal(barrier, inc=1, device_id=(lax.rem(r + d, nr), c), device_id_type=MESH)
        return carry

    def greet_col(d, carry):
        pl.semaphore_signal(barrier, inc=1, device_id=(r, lax.rem(c + d, nc)), device_id_type=MESH)
        return carry

    lax.fori_loop(1, nr, greet_row, 0)
    lax.fori_loop(1, nc, greet_col, 0)
    row8 = pl.multiple_of(128 * k + 8 * c, 8)
    pltpu.make_async_copy(fac1.at[:, pl.ds(row8, 8), pl.ds(lanes, 128)], pf.at[pl.ds(r * f1, f1)], pfr).start()
    pltpu.make_async_copy(fac2.at[:, pl.ds(row8, 8), pl.ds(lanes, 128)], pg.at[pl.ds(r * f2, f2)], pgr).start()
    for cp in small:
        cp.start()
    for b in range(ns):
        load_a(b).start()
    pl.semaphore_wait(barrier, nr + nc - 2)

    def send_pieces(fac, buf, count, rsem):
        def go(d, carry):
            r2 = lax.rem(r + d, nr)
            k2 = lax.rem(r2, 2)
            rows = pl.multiple_of(128 * k2 + 8 * c, 8)
            side = pl.multiple_of(128 * lax.rem(r2 // 2, 2), 128)
            remote(
                fac.at[:, pl.ds(rows, 8), pl.ds(side, 128)], buf.at[pl.ds(r * count, count)], s1, rsem, r2, c
            ).start()
            return carry

        lax.fori_loop(1, nr, go, 0)

    send_pieces(fac1, pf, f1, pfr)
    send_pieces(fac2, pg, f2, pgr)

    tile = lax.broadcasted_iota(jnp.int32, (8, 128), 1)
    at1 = jnp.zeros((8, 128), jnp.int32)
    at2 = jnp.zeros((8, 128), jnp.int32)
    for j in range(ids1.shape[0]):
        at1 = jnp.where(tile == ids1[j], j + 1, at1)
    for j in range(ids2.shape[0]):
        at2 = jnp.where(tile == ids2[j], j + 1, at2)
    in2 = jnp.where(at2 > 0, 1, 0)
    only1 = jnp.where(at1 > 0, 1, 0) - in2

    def lower(v):
        tot = jnp.zeros_like(v)
        for d in range(1, na):
            tot = tot + jnp.where(tile >= d * nc, pltpu.roll(v, d * nc, axis=1), 0)
        return tot

    def fold_tiles(v):
        tot = v
        for d in range(1, na):
            tot = tot + pltpu.roll(v, 128 - d * nc, axis=1)
        return tot

    def spread(v):
        tot = v
        for d in range(1, na):
            tot = tot + jnp.where(tile >= d * nc, pltpu.roll(v, d * nc, axis=1), 0)
        return tot

    count2 = spread(jnp.where(tile < nc, fold_tiles(in2), 0))
    rank = jnp.where(in2 > 0, lower(in2), count2 + lower(only1))
    line = lax.broadcasted_iota(jnp.int32, (8, 128), 0)
    t1 = jnp.zeros((8, 128), jnp.int32)
    t2 = jnp.zeros((8, 128), jnp.int32)
    ti = jnp.zeros((8, 128), jnp.int32)
    for a in range(n1):
        hit = jnp.logical_and(at1 > 0, rank == a)
        t1 = jnp.where(line == a, fold_tiles(jnp.where(hit, at1, 0)), t1)
        t2 = jnp.where(line == a, fold_tiles(jnp.where(hit, at2, 0)), t2)
        ti = jnp.where(line == a, fold_tiles(jnp.where(hit, tile // nc, 0)), ti)
    tab_v[0:8, :] = t1 - 1
    tab_v[8:16, :] = t2 - 1
    tab_v[16:24, :] = ti
    tab_v[24:32, :] = jnp.where(
        line == 0, jnp.where(at1 > 0, rank, -1), jnp.where(in2 > 0, rank, -1)
    )
    to_smem = pltpu.make_async_copy(tab_v, tab, lt)
    to_smem.start()
    for cp in small:
        cp.wait()
    first = jnp.where(jnp.logical_and(r == 0, c == 0), 1.0, 0.0).astype(F32)
    lt_v[...] = jnp.transpose(l_v[...])
    d1_v[...] = jnp.transpose(d1_v[...]) * first
    d2_v[...] = jnp.transpose(d2_v[...]) * first

    to_smem.wait()
    take(pf, pfr)
    take(pg, pgr)

    def pack(b, carry):
        def send(fg, cw):
            def one(c2, carry2):
                j = tab[(row1, row2)[fg] + b, c2]
                v = (pf, pg)[fg][jnp.maximum(j, 0)]
                st[fg, b, c2] = jnp.where(j >= 0, v, 0.0)
                return carry2

            lax.fori_loop(0, nc, one, 0)
            pltpu.make_async_copy(st.at[fg, b, c], cw.at[b, e, k, c], br.at[fg, b]).start()

            def go(d, carry2):
                c2 = lax.rem(c + d, nc)
                remote(st.at[fg, b, c2], cw.at[b, e, k, c], bs.at[fg], br.at[fg, b], r, c2).start()
                return carry2

            lax.fori_loop(1, nc, go, 0)

        send(0, cw1)

        @pl.when(b < n2)
        def _():
            send(1, cw2)

        return carry

    lax.fori_loop(0, n1, pack, 0)

    other = z + 1 - 2 * e
    for t in range(4):
        z2 = z if t < 2 else other
        k2 = k if t % 2 == 0 else 1 - k
        r2 = z2 * 2 + k2
        for a in range(n1):
            j1 = tab[row1 + a, r2]
            rps[t, a] = jnp.where(j1 >= 0, pf[jnp.maximum(j1, 0)], 0.0)
        for a in range(n2):
            j2 = tab[row2 + a, r2]
            rps[t, n1 + a] = jnp.where(j2 >= 0, pg[jnp.maximum(j2, 0)], 0.0)
        if t == 0:
            pltpu.make_async_copy(rps.at[t], rp.at[e * 2 + k], rr).start()
        else:
            remote(rps.at[t], rp.at[e * 2 + k], rs_, rr, r2, c).start()

    def ring(h):
        if h == 0:
            return x, y * SIDE + lax.rem(x + 1, SIDE), y * SIDE + lax.rem(x + SIDE - 1, SIDE)
        return y, lax.rem(y + 1, SIDE) * SIDE + x, lax.rem(y + SIDE - 1, SIDE) * SIDE + x

    half = SIDE // 2

    def part(a, h, who, lo, n):
        if h == 0:
            return acc.at[a, 0, pl.ds(lo, n), who]
        return acc.at[a, 1, who, pl.ds(lo, n)]

    def step_one(a):
        for h in range(2):
            u, right, left = ring(h)
            up, down, far = lax.rem(u + 1, SIDE), lax.rem(u + SIDE - 1, SIDE), lax.rem(u + 2, SIDE)
            remote(part(a, h, far, 0, half), hop.at[h, 0, a], r1s, r1r.at[h, 0, a], r, right).start()
            remote(part(a, h, far, half, half), hop.at[h, 1, a], r1s, r1r.at[h, 1, a], r, left).start()
            remote(
                part(a, h, up, half, half), fb.at[h, 0, a, pl.ds(half, half)], r1s, fbr.at[h, 0, a], r, right
            ).start()
            remote(
                part(a, h, down, 0, half), fb.at[h, 1, a, pl.ds(0, half)], r1s, fbr.at[h, 1, a], r, left
            ).start()

    def whole(cw, b):
        return jnp.concatenate([cw[b, 0].reshape(256, 128), cw[b, 1].reshape(256, 128)], axis=1)

    def slot(b):
        ff = whole(cw1, b)
        fh, fl = split(ff)
        w3[0:256, 0:256] = fh
        w3[256:512, 0:256] = fl
        w3[512:768, 0:256] = fh
        fll = dot3(ff, l_v[...])

        def put(hh):
            hhi, hlo = split(hh)
            w3[0:256, 256:512] = hhi
            w3[256:512, 256:512] = hlo
            w3[512:768, 256:512] = hhi

        @pl.when(b < n2)
        def _():
            put(whole(cw2, jnp.minimum(b, n2 - 1)) - fll)

        @pl.when(b >= n2)
        def _():
            put(-fll)

        col = tab[rowi + b, c]

        def rowstep(a, cols):
            ah, al = split(a_v[tab[rowi + a, r], col])
            got = mm(jnp.concatenate([ah, ah, al], axis=1), w3[:, 0:cols])
            for fg in range(cols // 256):
                u = n1 * fg + a
                g = got[:, fg * 256:fg * 256 + 256].reshape(2, SIDE, SIDE, 8, 256)

                @pl.when(b == 0)
                def _():
                    acc[u] = g

                @pl.when(b > 0)
                def _():
                    acc[u] += g

                @pl.when(b == n1 - 1)
                def _():
                    step_one(u)

        def both(a, carry):
            rowstep(a, 512)
            return carry

        def first_only(a, carry):
            rowstep(a, 256)
            return carry

        lax.fori_loop(0, n2, both, 0)
        if n2 < n1:
            lax.fori_loop(n2, n1, first_only, 0)

    def swap(cw, fg, b):
        mine = cw.at[b, e, k]
        take(mine, br.at[fg, b])
        remote(mine, mine, cs.at[fg], cr.at[fg, b], mate, c).start()
        remote(mine, mine, zxs.at[fg], zxr.at[fg, b], (z_down, z_up)[fg], c).start()

    def hand(cw, fg, b):
        got = cw.at[b, 1 - e, k]
        take(got, zxr.at[fg, b])
        remote(got, got, cs.at[fg], cr.at[fg, b], mate, c).start()

    def slots(b, carry):
        @pl.when(b < n1)
        def _():
            swap(cw1, 0, b)

        @pl.when(b < n2)
        def _():
            swap(cw2, 1, b)

        @pl.when(jnp.logical_and(b > 0, b <= n1))
        def _():
            hand(cw1, 0, b - 1)

        @pl.when(jnp.logical_and(b > 0, b <= n2))
        def _():
            hand(cw2, 1, b - 1)

        @pl.when(b > 1)
        def _():
            take(cw1.at[b - 2, :, 1 - k], cr.at[0, b - 2])

            @pl.when(b - 2 < n2)
            def _():
                take(cw2.at[b - 2, :, 1 - k], cr.at[1, b - 2])

            slot(b - 2)

        return carry

    for b in range(ns):
        load_a(b).wait()
    lax.fori_loop(0, n1 + 2, slots, 0)

    def step_two(a, carry):
        for h in range(2):
            u, right, left = ring(h)
            up, down = lax.rem(u + 1, SIDE), lax.rem(u + SIDE - 1, SIDE)
            take(hop.at[h, 0, a], r1r.at[h, 0, a])
            hopped[h, 0, a] = hop[h, 0, a] + part(a, h, up, 0, half)[...]
            remote(
                hopped.at[h, 0, a], fb.at[h, 0, a, pl.ds(0, half)], r2s, fbr.at[h, 0, a], r, right
            ).start()
            take(hop.at[h, 1, a], r1r.at[h, 1, a])
            hopped[h, 1, a] = hop[h, 1, a] + part(a, h, down, half, half)[...]
            remote(
                hopped.at[h, 1, a], fb.at[h, 1, a, pl.ds(half, half)], r2s, fbr.at[h, 1, a], r, left
            ).start()
        return carry

    lax.fori_loop(0, nu, step_two, 0)

    take(rp, rr)
    frb[...] = jnp.zeros_like(frb)
    grb[...] = jnp.zeros_like(grb)
    x1b[...] = jnp.zeros_like(x1b)
    x2b[...] = jnp.zeros_like(x2b)
    for h in range(2):
        for g in range(2):
            for a in range(n1):
                frb[a * 16 + h * 8:a * 16 + h * 8 + 8, g * 128:g * 128 + 128] = rp[g * 2 + h, a]
            for a in range(n2):
                grb[a * 16 + h * 8:a * 16 + h * 8 + 8, g * 128:g * 128 + 128] = rp[g * 2 + h, n1 + a]

    def second(a, carry):
        for h in range(2):
            u = ring(h)[0]
            take(fb.at[h, 0, a], fbr.at[h, 0, a])
            take(fb.at[h, 1, a], fbr.at[h, 1, a])
            ysum[h, a] = part(a, h, u, 0, SIDE)[...] + (fb[h, 0, a] + fb[h, 1, a])
            v = y if h == 0 else x
            for d in range(1, SIDE):
                v2 = lax.rem(v + d, SIDE)
                col = v2 * SIDE + x if h == 0 else y * SIDE + v2
                remote(ysum.at[h, a, v2], zin.at[h, a, d - 1], zs, zr.at[h, a], r, col).start()
        return carry

    lax.fori_loop(0, nu, second, 0)

    def gather(fg, buf):
        def one(a, carry):
            u = n1 * fg + a
            for h in range(2):
                v = y if h == 0 else x
                take(zin.at[h, u], zr.at[h, u])
                tot = ysum[h, u, v] + (zin[h, u, 0] + zin[h, u, 1] + zin[h, u, 2])
                buf[pl.ds(pl.multiple_of(a * 16 + h * 8, 8), 8), :] = tot
            return carry

        lax.fori_loop(0, (n1, n2)[fg], one, 0)

    gather(0, x1b)
    x1 = x1b[...]
    d1t = dot3(jnp.transpose(x1), frb[...]) + d1_v[...]
    m_v[0] = d1t.reshape(nc, 2, 8, 256)
    jt = dot3(lt_v[...], d1t) - dot3(jnp.transpose(grb[...]), x1)
    m_v[1] = jt.reshape(nc, 2, 8, 256)

    def fold(t):
        return remote(m_v.at[t, :, 1 - k], rx.at[t], es, er.at[t], mate, c)

    fold(0).start()
    fold(1).start()
    base = dot3(jt, l_v[...]) + d2_v[...]
    gather(1, x2b)
    et = dot3(jnp.transpose(x2b[...]), grb[...]) + base
    m_v[2] = et.reshape(nc, 2, 8, 256)
    fold(2).start()

    def send_term(t):
        take(rx.at[t], er.at[t])
        n_v[t] = m_v[t, :, k] + rx[t]
        pltpu.make_async_copy(n_v.at[t, c], q_v.at[t, c], qr.at[t]).start()

        def go(d, carry):
            c2 = lax.rem(c + d, nc)
            remote(n_v.at[t, c2], q_v.at[t, c], qs, qr.at[t], r, c2).start()
            return carry

        lax.fori_loop(1, nc, go, 0)

    for t in range(3):
        send_term(t)

    lane = lax.broadcasted_iota(jnp.int32, (16, 128), 1) // 16
    for c2 in range(nc):
        blk, off = c2 // 8, c2 % 8
        for q in range(width // 128):
            val = jnp.zeros((16, 128), F32)
            for g in range(8):
                u = q * 8 + g
                if u < nu:
                    buf, a = (x1b, u) if u < n1 else (x2b, u - n1)
                    src = buf[a * 16:a * 16 + 16, blk * 128:blk * 128 + 128]
                    shift = (16 * (g - off)) % 128
                    if shift:
                        src = pltpu.roll(src, shift, axis=1)
                    val = jnp.where(lane == g, src, val)
            st2[c2, :, :, q * 128:(q + 1) * 128] = val.reshape(2, 8, 128)
    pltpu.make_async_copy(st2.at[c], rb.at[:, c], tr).start()

    def send_cols(d, carry):
        c2 = lax.rem(c + d, nc)
        remote(st2.at[c2], rb.at[:, c], ts, tr, r, c2).start()
        return carry

    lax.fori_loop(1, nc, send_cols, 0)

    def send_sum(t):
        take(q_v.at[t], qr.at[t])
        tot = q_v[t, 0]
        for i in range(1, nc):
            tot = tot + q_v[t, i]
        s_v[t] = tot
        pltpu.make_async_copy(s_v.at[t], u_v.at[t, z], ur.at[t]).start()

        def go(d, carry):
            z2 = lax.rem(z + d, nz)
            remote(s_v.at[t], u_v.at[t, z], us, ur.at[t], z2 * 2 + k, c).start()
            return carry

        lax.fori_loop(1, nz, go, 0)

    for t in range(3):
        send_sum(t)

    take(rb, tr)
    cols = jnp.transpose(rb[...].reshape(256, width))
    for fg in range(2):
        for a in range(na):
            slot_of = tab[(rowp, rowq)[fg], a * nr + r]
            val = jnp.zeros((16, 256), F32)
            for i in range((n1, n2)[fg]):
                lo = (n1 * fg + i) * 16
                val = jnp.where(slot_of == i, -cols[lo:lo + 16, :], val)
            lo = (na * fg + a) * 16
            out[lo:lo + 16, :] = val

    for t in range(3):
        take(u_v.at[t], ur.at[t])
        tot = u_v[t, 0]
        for i in range(1, nz):
            tot = tot + u_v[t, i]
        w_v[k, t] = tot
    last = remote(w_v.at[k], w_v.at[k], vs, vr, mate, c)
    last.start()
    take(w_v.at[k], vr)
    for h in range(2):
        lo = na * 32 + h * 8
        out[lo:lo + 8, :] = w_v[h, 0]
        out[lo + 16:lo + 24, :] = -w_v[h, 1]
        out[lo + 32:lo + 40, :] = w_v[h, 2]

    take(pf.at[pl.ds(0, (nr - 1) * f1)], s1)
    take(pg.at[pl.ds(0, (nr - 1) * f2)], s1)
    for fg, cw, n in ((0, cw1, n1), (1, cw2, n2)):
        take(st.at[fg, pl.ds(0, n), pl.ds(0, nc - 1)], bs.at[fg])
        take(cw.at[:, :, 0], cs.at[fg])
        take(cw.at[:, 0, 0], zxs.at[fg])
    take(rp.at[pl.ds(0, 3)], rs_)
    take(fb, r1s)
    take(hop, r2s)
    take(zin, zs)
    take(rb.at[:, pl.ds(0, nc - 1)], ts)
    take(rx, es)
    take(q_v.at[:, pl.ds(0, nc - 1)], qs)
    take(u_v.at[:, pl.ds(0, nz - 1)], us)
    take(w_v.at[0], vs)


def part_out(rows, o, p1, p2, g1, g2, g3):
    p1[...] = o[0:rows, :]
    p2[...] = o[rows:2 * rows, :]
    for n, g in enumerate((g1, g2, g3)):
        g[...] = o[2 * rows + 16 * n:2 * rows + 16 * n + 16, :]


def fused(n1, n2, ident, struct_first, struct_second, inverse, factor_first, factor_second, link_factor, dinv_first, dinv_second):
    nr = lax.axis_size("row")
    nc = lax.axis_size("col")
    na, ns, ext, _ = inverse.shape
    f1, f2 = factor_first.shape[0], factor_second.shape[0]
    assert nr == nc == SIDE * SIDE and na == ns and na * nc <= 128 and n1 <= 8
    nu = n1 + n2
    nz = nr // 2
    width = -(-nu * 16 // 128) * 128
    deep = -(-n1 * 16 // 128) * 128
    rows = na * 16
    any_spec = pl.BlockSpec(memory_space=pl.ANY)
    vm = lambda *s: pltpu.VMEM(s, F32)
    dma = pltpu.SemaphoreType.DMA
    half = SIDE // 2
    return pl.pallas_call(
        functools.partial(kernel, nr, nc, na, ns, f1, f2, n1, n2, width),
        out_shape=jax.ShapeDtypeStruct((2 * rows + 48, 256), F32),
        in_specs=[pl.BlockSpec(memory_space=pltpu.SMEM)] * 2 + [any_spec] * 6,
        out_specs=pl.BlockSpec(memory_space=pltpu.VMEM),
        scratch_shapes=[
            pltpu.VMEM((32, 128), jnp.int32), pltpu.SMEM((32, 128), jnp.int32),
            vm(na, ns, 256, 256), vm(256, 256), vm(256, 256), vm(256, 256), vm(256, 256),
            vm(nr * f1, 8, 128), vm(nr * f2, 8, 128), vm(4, nu, 8, 128), vm(4, nu, 8, 128),
            vm(2, n1, nc, 8, 128), vm(n1, 2, 2, nc, 8, 128), vm(n2, 2, 2, nc, 8, 128),
            pltpu.VMEM((768, 512), BF16),
            vm(nu, 2, SIDE, SIDE, 8, 256),
            vm(2, 2, nu, half, 8, 256), vm(2, 2, nu, half, 8, 256),
            vm(2, 2, nu, SIDE, 8, 256), vm(2, nu, SIDE, 8, 256),
            vm(2, nu, SIDE - 1, 8, 256),
            vm(deep, 256), vm(deep, 256), vm(deep, 256), vm(deep, 256),
            vm(nc, 2, 8, width), vm(2, nc, 8, width),
            vm(3, nc, 2, 8, 256), vm(3, nc, 8, 256), vm(3, nc, 8, 256), vm(3, nc, 8, 256),
            vm(3, 8, 256), vm(3, nz, 8, 256), vm(2, 3, 8, 256),
            dma((ns,)), dma((3,)), dma, dma, dma, dma, dma, dma,
            dma((2,)), dma((2, n1)), dma((2,)), dma((2, n1)), dma((2,)), dma((2, n1)),
            dma, dma((2, 2, nu)), dma, dma((2, 2, nu)), dma, dma((2, nu)),
            dma, dma, dma, dma((3,)), dma, dma((3,)), dma, dma((3,)), dma, dma,
        ],
        compiler_params=pltpu.CompilerParams(
            collective_id=ident, has_side_effects=True, vmem_limit_bytes=56 * 1024 * 1024
        ),
    )(struct_first, struct_second, inverse, factor_first, factor_second, link_factor, dinv_first, dinv_second)


def body(inverse, struct_first, struct_second, factor_first, factor_second, link_factor, dinv_first, dinv_second):
    na, _, ns, _, ext, _ = inverse.shape
    rows = na * 16
    args = (
        struct_first, struct_second, inverse.reshape(na, ns, ext, ext),
        factor_first, factor_second, link_factor, dinv_first, dinv_second,
    )
    o = fused(na, na, 0, *args)
    small = jax.ShapeDtypeStruct((16, 256), F32)
    tall = jax.ShapeDtypeStruct((rows, 256), F32)
    p1, p2, g1, g2, g3 = pl.pallas_call(
        functools.partial(part_out, rows),
        out_shape=(tall, tall, small, small, small),
    )(o)
    panel = lambda v: jnp.swapaxes(v.reshape(na, 1, 16, 256), 2, 3)
    turn = lambda v: jnp.swapaxes(v, 0, 1)
    return (panel(p1), turn(g1), panel(p2), turn(g2), turn(g3))


def solution(mesh):
    placed = (
        P(None, "row", None, "col", None, None),
        P(),
        P(),
        P("row", None, None),
        P("row", None, None),
        P(),
        P(),
        P(),
    )
    return jax.shard_map(
        body,
        mesh=mesh,
        in_specs=placed,
        out_specs=(
            P(None, "row", None, "col"),
            P(None, "col"),
            P(None, "row", None, "col"),
            P(None, "col"),
            P(None, "col"),
        ),
        check_vma=False,
    )
```

```python
import functools

import jax
import jax.numpy as jnp
from jax import lax
from jax.experimental import pallas as pl
from jax.experimental.pallas import tpu as pltpu
from jax.sharding import PartitionSpec as P

MESH = pl.DeviceIdType.MESH
SIDE = 4
TIGHT = (4, 3)
F32 = jnp.float32
BF16 = jnp.bfloat16


def split(v):
    hi = v.astype(BF16)
    return hi, (v - hi.astype(F32)).astype(BF16)


def mm(p, q):
    return jnp.dot(p, q, preferred_element_type=F32)


def dot3(p, q):
    ph, plo = split(p)
    qh, qlo = split(q)
    return mm(ph, qh) + (mm(ph, qlo) + mm(plo, qh))


def kernel(
    nr, nc, na, ns, f1, f2, n1, n2, width,
    ids1, ids2, inv, fac1, fac2, link, dinv1, dinv2,
    out,
    tab_v, tab, a_v, l_v, d1_v, d2_v, lt_v,
    pf, pg, rps, rp, st, cw1, cw2, lhs, w3, acc,
    hop, hopped, fb, ysum, zin, x1b, x2b, frb, grb,
    st2, rb, m_v, rx, n_v, q_v, s_v, u_v, w_v,
    ld, lds, lt, s1, pfr, pgr, rs_, rr, bs, br, zxs, zxr, cs, cr,
    r1s, r1r, r2s, fbr, zs, zr, ts, tr, es, er, qs, qr, us, ur, vs, vr,
):
    r = lax.axis_index("row")
    c = lax.axis_index("col")
    k = lax.rem(r, 2)
    z = r // 2
    nz = nr // 2
    y = c // SIDE
    x = lax.rem(c, SIDE)
    e = lax.rem(z, 2)
    mate = z * 2 + (1 - k)
    z_up = lax.rem(z + 1, nz) * 2 + k
    z_down = lax.rem(z + nz - 1, nz) * 2 + k
    lanes = pl.multiple_of(128 * e, 128)
    nu = n1 + n2
    row1, row2, rowi, rowp, rowq = 0, 8, 16, 24, 25

    def remote(src, dst, ss, rs, row, col):
        return pltpu.make_async_remote_copy(
            src_ref=src, dst_ref=dst, send_sem=ss, recv_sem=rs,
            device_id=(row, col), device_id_type=MESH,
        )

    def take(ref, sem):
        pltpu.make_async_copy(ref, ref, sem).wait()

    def load_a(b):
        return pltpu.make_async_copy(inv.at[:, b], a_v.at[:, b], ld.at[b])

    small = [
        pltpu.make_async_copy(link, l_v, lds.at[0]),
        pltpu.make_async_copy(dinv1, d1_v, lds.at[1]),
        pltpu.make_async_copy(dinv2, d2_v, lds.at[2]),
    ]
    barrier = pltpu.get_barrier_semaphore()

    def greet_row(d, carry):
        pl.semaphore_signal(barrier, inc=1, device_id=(lax.rem(r + d, nr), c), device_id_type=MESH)
        return carry

    def greet_col(d, carry):
        pl.semaphore_signal(barrier, inc=1, device_id=(r, lax.rem(c + d, nc)), device_id_type=MESH)
        return carry

    lax.fori_loop(1, nr, greet_row, 0)
    lax.fori_loop(1, nc, greet_col, 0)
    row8 = pl.multiple_of(128 * k + 8 * c, 8)
    pltpu.make_async_copy(fac1.at[:, pl.ds(row8, 8), pl.ds(lanes, 128)], pf.at[pl.ds(r * f1, f1)], pfr).start()
    pltpu.make_async_copy(fac2.at[:, pl.ds(row8, 8), pl.ds(lanes, 128)], pg.at[pl.ds(r * f2, f2)], pgr).start()
    for cp in small:
        cp.start()
    for b in range(ns):
        load_a(b).start()
    pl.semaphore_wait(barrier, nr + nc - 2)

    def send_pieces(fac, buf, count, rsem):
        def go(d, carry):
            r2 = lax.rem(r + d, nr)
            k2 = lax.rem(r2, 2)
            rows = pl.multiple_of(128 * k2 + 8 * c, 8)
            side = pl.multiple_of(128 * lax.rem(r2 // 2, 2), 128)
            remote(
                fac.at[:, pl.ds(rows, 8), pl.ds(side, 128)], buf.at[pl.ds(r * count, count)], s1, rsem, r2, c
            ).start()
            return carry

        lax.fori_loop(1, nr, go, 0)

    send_pieces(fac1, pf, f1, pfr)
    send_pieces(fac2, pg, f2, pgr)

    tile = lax.broadcasted_iota(jnp.int32, (8, 128), 1)
    at1 = jnp.zeros((8, 128), jnp.int32)
    at2 = jnp.zeros((8, 128), jnp.int32)
    for j in range(ids1.shape[0]):
        at1 = jnp.where(tile == ids1[j], j + 1, at1)
    for j in range(ids2.shape[0]):
        at2 = jnp.where(tile == ids2[j], j + 1, at2)
    in2 = jnp.where(at2 > 0, 1, 0)
    only1 = jnp.where(at1 > 0, 1, 0) - in2

    def lower(v):
        tot = jnp.zeros_like(v)
        for d in range(1, na):
            tot = tot + jnp.where(tile >= d * nc, pltpu.roll(v, d * nc, axis=1), 0)
        return tot

    def fold_tiles(v):
        tot = v
        for d in range(1, na):
            tot = tot + pltpu.roll(v, 128 - d * nc, axis=1)
        return tot

    def spread(v):
        tot = v
        for d in range(1, na):
            tot = tot + jnp.where(tile >= d * nc, pltpu.roll(v, d * nc, axis=1), 0)
        return tot

    count2 = spread(jnp.where(tile < nc, fold_tiles(in2), 0))
    rank = jnp.where(in2 > 0, lower(in2), count2 + lower(only1))
    line = lax.broadcasted_iota(jnp.int32, (8, 128), 0)
    t1 = jnp.zeros((8, 128), jnp.int32)
    t2 = jnp.zeros((8, 128), jnp.int32)
    ti = jnp.zeros((8, 128), jnp.int32)
    for a in range(n1):
        hit = jnp.logical_and(at1 > 0, rank == a)
        t1 = jnp.where(line == a, fold_tiles(jnp.where(hit, at1, 0)), t1)
        t2 = jnp.where(line == a, fold_tiles(jnp.where(hit, at2, 0)), t2)
        ti = jnp.where(line == a, fold_tiles(jnp.where(hit, tile // nc, 0)), ti)
    tab_v[0:8, :] = t1 - 1
    tab_v[8:16, :] = t2 - 1
    tab_v[16:24, :] = ti
    tab_v[24:32, :] = jnp.where(
        line == 0, jnp.where(at1 > 0, rank, -1), jnp.where(in2 > 0, rank, -1)
    )
    to_smem = pltpu.make_async_copy(tab_v, tab, lt)
    to_smem.start()
    for cp in small:
        cp.wait()
    first = jnp.where(jnp.logical_and(r == 0, c == 0), 1.0, 0.0).astype(F32)
    lt_v[...] = jnp.transpose(l_v[...])
    d1_v[...] = jnp.transpose(d1_v[...]) * first
    d2_v[...] = jnp.transpose(d2_v[...]) * first

    to_smem.wait()
    take(pf, pfr)
    take(pg, pgr)

    def pack(b, carry):
        def send(fg, cw):
            def one(c2, carry2):
                j = tab[(row1, row2)[fg] + b, c2]
                v = (pf, pg)[fg][jnp.maximum(j, 0)]
                st[fg, b, c2] = jnp.where(j >= 0, v, 0.0)
                return carry2

            lax.fori_loop(0, nc, one, 0)
            pltpu.make_async_copy(st.at[fg, b, c], cw.at[b, e, k, c], br.at[fg, b]).start()

            def go(d, carry2):
                c2 = lax.rem(c + d, nc)
                remote(st.at[fg, b, c2], cw.at[b, e, k, c], bs.at[fg], br.at[fg, b], r, c2).start()
                return carry2

            lax.fori_loop(1, nc, go, 0)

        send(0, cw1)

        @pl.when(b < n2)
        def _():
            send(1, cw2)

        return carry

    lax.fori_loop(0, n1, pack, 0)

    other = z + 1 - 2 * e
    for t in range(4):
        z2 = z if t < 2 else other
        k2 = k if t % 2 == 0 else 1 - k
        r2 = z2 * 2 + k2
        for a in range(n1):
            j1 = tab[row1 + a, r2]
            rps[t, a] = jnp.where(j1 >= 0, pf[jnp.maximum(j1, 0)], 0.0)
        for a in range(n2):
            j2 = tab[row2 + a, r2]
            rps[t, n1 + a] = jnp.where(j2 >= 0, pg[jnp.maximum(j2, 0)], 0.0)
        if t == 0:
            pltpu.make_async_copy(rps.at[t], rp.at[e * 2 + k], rr).start()
        else:
            remote(rps.at[t], rp.at[e * 2 + k], rs_, rr, r2, c).start()

    def ring(h):
        if h == 0:
            return x, y * SIDE + lax.rem(x + 1, SIDE), y * SIDE + lax.rem(x + SIDE - 1, SIDE)
        return y, lax.rem(y + 1, SIDE) * SIDE + x, lax.rem(y + SIDE - 1, SIDE) * SIDE + x

    half = SIDE // 2

    def part(a, h, who, lo, n):
        if h == 0:
            return acc.at[a, 0, pl.ds(lo, n), who]
        return acc.at[a, 1, who, pl.ds(lo, n)]

    def step_one(a):
        for h in range(2):
            u, right, left = ring(h)
            up, down, far = lax.rem(u + 1, SIDE), lax.rem(u + SIDE - 1, SIDE), lax.rem(u + 2, SIDE)
            remote(part(a, h, far, 0, half), hop.at[h, 0, a], r1s, r1r.at[h, 0, a], r, right).start()
            remote(part(a, h, far, half, half), hop.at[h, 1, a], r1s, r1r.at[h, 1, a], r, left).start()
            remote(
                part(a, h, up, half, half), fb.at[h, 0, a, pl.ds(half, half)], r1s, fbr.at[h, 0, a], r, right
            ).start()
            remote(
                part(a, h, down, 0, half), fb.at[h, 1, a, pl.ds(0, half)], r1s, fbr.at[h, 1, a], r, left
            ).start()

    def whole(cw, b):
        return jnp.concatenate([cw[b, 0].reshape(256, 128), cw[b, 1].reshape(256, 128)], axis=1)

    def weights(b):
        ff = whole(cw1, b)
        fh, fl = split(ff)
        w3[b, 0:256, 0:256] = fh
        w3[b, 256:512, 0:256] = fl
        w3[b, 512:768, 0:256] = fh
        fll = dot3(ff, l_v[...])

        def put(hh):
            hhi, hlo = split(hh)
            w3[b, 0:256, 256:512] = hhi
            w3[b, 256:512, 256:512] = hlo
            w3[b, 512:768, 256:512] = hhi

        @pl.when(b < n2)
        def _():
            put(whole(cw2, jnp.minimum(b, n2 - 1)) - fll)

        @pl.when(b >= n2)
        def _():
            put(-fll)

    def term(a, b, lo, cols):
        v = lhs[b, a]
        return mm(jnp.concatenate([v[:, 0:256], v[:, 0:256], v[:, 256:512]], axis=1), w3[b, :, lo:lo + cols])

    early = n1 - 2

    def part_sums(b):
        def rowstep(a, cols):
            got = term(a, b, 0, cols)
            for fg in range(cols // 256):
                u = n1 * fg + a
                g = got[:, fg * 256:fg * 256 + 256].reshape(2, SIDE, SIDE, 8, 256)

                @pl.when(b == 0)
                def _():
                    acc[u] = g

                @pl.when(b > 0)
                def _():
                    acc[u] += g

        def both(a, carry):
            rowstep(a, 512)
            return carry

        def first_only(a, carry):
            rowstep(a, 256)
            return carry

        lax.fori_loop(0, n2, both, 0)
        if n2 < n1:
            lax.fori_loop(n2, n1, first_only, 0)

    def finish(fg):
        def one(a, carry):
            got = term(a, early, 256 * fg, 256) + term(a, early + 1, 256 * fg, 256)
            acc[n1 * fg + a] += got.reshape(2, SIDE, SIDE, 8, 256)
            step_one(n1 * fg + a)
            return carry

        lax.fori_loop(0, (n1, n2)[fg], one, 0)

    def swap(cw, fg, b):
        mine = cw.at[b, e, k]
        take(mine, br.at[fg, b])
        remote(mine, mine, cs.at[fg], cr.at[fg, b], mate, c).start()
        remote(mine, mine, zxs.at[fg], zxr.at[fg, b], (z_down, z_up)[fg], c).start()

    def hand(cw, fg, b):
        got = cw.at[b, 1 - e, k]
        take(got, zxr.at[fg, b])
        remote(got, got, cs.at[fg], cr.at[fg, b], mate, c).start()

    def slots(b, carry):
        @pl.when(b < n1)
        def _():
            swap(cw1, 0, b)

        @pl.when(b < n2)
        def _():
            swap(cw2, 1, b)

        @pl.when(jnp.logical_and(b > 0, b <= n1))
        def _():
            hand(cw1, 0, b - 1)

        @pl.when(jnp.logical_and(b > 0, b <= n2))
        def _():
            hand(cw2, 1, b - 1)

        @pl.when(b > 1)
        def _():
            take(cw1.at[b - 2, :, 1 - k], cr.at[0, b - 2])

            @pl.when(b - 2 < n2)
            def _():
                take(cw2.at[b - 2, :, 1 - k], cr.at[1, b - 2])

            weights(b - 2)

            @pl.when(b - 2 < early)
            def _():
                part_sums(b - 2)

        return carry

    for b in range(ns):
        load_a(b).wait()

    def cast(i, carry):
        a, b = i // n1, lax.rem(i, n1)
        ah, al = split(a_v[tab[rowi + a, r], tab[rowi + b, c]])
        lhs[b, a, :, 0:256] = ah
        lhs[b, a, :, 256:512] = al
        return carry

    lax.fori_loop(0, n1 * n1, cast, 0)
    lax.fori_loop(0, n1 + 2, slots, 0)
    finish(0)
    finish(1)

    def step_two(a, carry):
        for h in range(2):
            u, right, left = ring(h)
            up, down = lax.rem(u + 1, SIDE), lax.rem(u + SIDE - 1, SIDE)
            take(hop.at[h, 0, a], r1r.at[h, 0, a])
            hopped[h, 0, a] = hop[h, 0, a] + part(a, h, up, 0, half)[...]
            remote(
                hopped.at[h, 0, a], fb.at[h, 0, a, pl.ds(0, half)], r2s, fbr.at[h, 0, a], r, right
            ).start()
            take(hop.at[h, 1, a], r1r.at[h, 1, a])
            hopped[h, 1, a] = hop[h, 1, a] + part(a, h, down, half, half)[...]
            remote(
                hopped.at[h, 1, a], fb.at[h, 1, a, pl.ds(half, half)], r2s, fbr.at[h, 1, a], r, left
            ).start()
        return carry

    lax.fori_loop(0, nu, step_two, 0)

    take(rp, rr)
    frb[...] = jnp.zeros_like(frb)
    grb[...] = jnp.zeros_like(grb)
    x1b[...] = jnp.zeros_like(x1b)
    x2b[...] = jnp.zeros_like(x2b)
    for h in range(2):
        for g in range(2):
            for a in range(n1):
                frb[a * 16 + h * 8:a * 16 + h * 8 + 8, g * 128:g * 128 + 128] = rp[g * 2 + h, a]
            for a in range(n2):
                grb[a * 16 + h * 8:a * 16 + h * 8 + 8, g * 128:g * 128 + 128] = rp[g * 2 + h, n1 + a]

    def second(a, carry):
        for h in range(2):
            u = ring(h)[0]
            take(fb.at[h, 0, a], fbr.at[h, 0, a])
            take(fb.at[h, 1, a], fbr.at[h, 1, a])
            ysum[h, a] = part(a, h, u, 0, SIDE)[...] + (fb[h, 0, a] + fb[h, 1, a])
            v = y if h == 0 else x
            for d in range(1, SIDE):
                v2 = lax.rem(v + d, SIDE)
                col = v2 * SIDE + x if h == 0 else y * SIDE + v2
                remote(ysum.at[h, a, v2], zin.at[h, a, d - 1], zs, zr.at[h, a], r, col).start()
        return carry

    lax.fori_loop(0, nu, second, 0)

    def gather(fg, buf):
        def one(a, carry):
            u = n1 * fg + a
            for h in range(2):
                v = y if h == 0 else x
                take(zin.at[h, u], zr.at[h, u])
                tot = ysum[h, u, v] + (zin[h, u, 0] + zin[h, u, 1] + zin[h, u, 2])
                buf[pl.ds(pl.multiple_of(a * 16 + h * 8, 8), 8), :] = tot
            return carry

        lax.fori_loop(0, (n1, n2)[fg], one, 0)

    gather(0, x1b)
    x1 = x1b[...]
    d1t = dot3(jnp.transpose(x1), frb[...]) + d1_v[...]
    m_v[0] = d1t.reshape(nc, 2, 8, 256)
    jt = dot3(lt_v[...], d1t) - dot3(jnp.transpose(grb[...]), x1)
    m_v[1] = jt.reshape(nc, 2, 8, 256)

    def fold(t):
        return remote(m_v.at[t, :, 1 - k], rx.at[t], es, er.at[t], mate, c)

    fold(0).start()
    fold(1).start()
    base = dot3(jt, l_v[...]) + d2_v[...]
    gather(1, x2b)
    et = dot3(jnp.transpose(x2b[...]), grb[...]) + base
    m_v[2] = et.reshape(nc, 2, 8, 256)
    fold(2).start()

    def send_term(t):
        take(rx.at[t], er.at[t])
        n_v[t] = m_v[t, :, k] + rx[t]
        pltpu.make_async_copy(n_v.at[t, c], q_v.at[t, c], qr.at[t]).start()

        def go(d, carry):
            c2 = lax.rem(c + d, nc)
            remote(n_v.at[t, c2], q_v.at[t, c], qs, qr.at[t], r, c2).start()
            return carry

        lax.fori_loop(1, nc, go, 0)

    for t in range(3):
        send_term(t)

    lane = lax.broadcasted_iota(jnp.int32, (16, 128), 1) // 16
    for c2 in range(nc):
        blk, off = c2 // 8, c2 % 8
        for q in range(width // 128):
            val = jnp.zeros((16, 128), F32)
            for g in range(8):
                u = q * 8 + g
                if u < nu:
                    buf, a = (x1b, u) if u < n1 else (x2b, u - n1)
                    src = buf[a * 16:a * 16 + 16, blk * 128:blk * 128 + 128]
                    shift = (16 * (g - off)) % 128
                    if shift:
                        src = pltpu.roll(src, shift, axis=1)
                    val = jnp.where(lane == g, src, val)
            st2[c2, :, :, q * 128:(q + 1) * 128] = val.reshape(2, 8, 128)
    pltpu.make_async_copy(st2.at[c], rb.at[:, c], tr).start()

    def send_cols(d, carry):
        c2 = lax.rem(c + d, nc)
        remote(st2.at[c2], rb.at[:, c], ts, tr, r, c2).start()
        return carry

    lax.fori_loop(1, nc, send_cols, 0)

    def send_sum(t):
        take(q_v.at[t], qr.at[t])
        tot = q_v[t, 0]
        for i in range(1, nc):
            tot = tot + q_v[t, i]
        s_v[t] = tot
        pltpu.make_async_copy(s_v.at[t], u_v.at[t, z], ur.at[t]).start()

        def go(d, carry):
            z2 = lax.rem(z + d, nz)
            remote(s_v.at[t], u_v.at[t, z], us, ur.at[t], z2 * 2 + k, c).start()
            return carry

        lax.fori_loop(1, nz, go, 0)

    for t in range(3):
        send_sum(t)

    take(rb, tr)
    cols = jnp.transpose(rb[...].reshape(256, width))
    for fg in range(2):
        for a in range(na):
            slot_of = tab[(rowp, rowq)[fg], a * nr + r]
            val = jnp.zeros((16, 256), F32)
            for i in range((n1, n2)[fg]):
                lo = (n1 * fg + i) * 16
                val = jnp.where(slot_of == i, -cols[lo:lo + 16, :], val)
            lo = (na * fg + a) * 16
            out[lo:lo + 16, :] = val

    for t in range(3):
        take(u_v.at[t], ur.at[t])
        tot = u_v[t, 0]
        for i in range(1, nz):
            tot = tot + u_v[t, i]
        w_v[k, t] = tot
    last = remote(w_v.at[k], w_v.at[k], vs, vr, mate, c)
    last.start()
    take(w_v.at[k], vr)
    for h in range(2):
        lo = na * 32 + h * 8
        out[lo:lo + 8, :] = w_v[h, 0]
        out[lo + 16:lo + 24, :] = -w_v[h, 1]
        out[lo + 32:lo + 40, :] = w_v[h, 2]

    take(pf.at[pl.ds(0, (nr - 1) * f1)], s1)
    take(pg.at[pl.ds(0, (nr - 1) * f2)], s1)
    for fg, cw, n in ((0, cw1, n1), (1, cw2, n2)):
        take(st.at[fg, pl.ds(0, n), pl.ds(0, nc - 1)], bs.at[fg])
        take(cw.at[:, :, 0], cs.at[fg])
        take(cw.at[:, 0, 0], zxs.at[fg])
    take(rp.at[pl.ds(0, 3)], rs_)
    take(fb, r1s)
    take(hop, r2s)
    take(zin, zs)
    take(rb.at[:, pl.ds(0, nc - 1)], ts)
    take(rx, es)
    take(q_v.at[:, pl.ds(0, nc - 1)], qs)
    take(u_v.at[:, pl.ds(0, nz - 1)], us)
    take(w_v.at[0], vs)


def spread_fits(n, ids1, ids2, out):
    lane = lax.broadcasted_iota(jnp.int32, (8, 128), 1)
    bad = jnp.zeros((8, 128), F32)
    for ids, most in ((ids1, TIGHT[0]), (ids2, TIGHT[1])):
        count = jnp.zeros((8, 128), F32)
        for j in range(ids.shape[0]):
            count = count + jnp.where(lane == lax.rem(ids[j], n), 1.0, 0.0)
        bad = jnp.maximum(bad, count - most)
    out[0] = jnp.where(jnp.max(bad) > 0.5, 0, 1)


def part_out(rows, o, p1, p2, g1, g2, g3):
    p1[...] = o[0:rows, :]
    p2[...] = o[rows:2 * rows, :]
    for n, g in enumerate((g1, g2, g3)):
        g[...] = o[2 * rows + 16 * n:2 * rows + 16 * n + 16, :]


def fused(n1, n2, ident, struct_first, struct_second, inverse, factor_first, factor_second, link_factor, dinv_first, dinv_second):
    nr = lax.axis_size("row")
    nc = lax.axis_size("col")
    na, ns, ext, _ = inverse.shape
    f1, f2 = factor_first.shape[0], factor_second.shape[0]
    assert nr == nc == SIDE * SIDE and na == ns and na * nc <= 128 and n1 <= 8
    nu = n1 + n2
    nz = nr // 2
    width = -(-nu * 16 // 128) * 128
    deep = -(-n1 * 16 // 128) * 128
    rows = na * 16
    any_spec = pl.BlockSpec(memory_space=pl.ANY)
    vm = lambda *s: pltpu.VMEM(s, F32)
    dma = pltpu.SemaphoreType.DMA
    half = SIDE // 2
    return pl.pallas_call(
        functools.partial(kernel, nr, nc, na, ns, f1, f2, n1, n2, width),
        out_shape=jax.ShapeDtypeStruct((2 * rows + 48, 256), F32),
        in_specs=[pl.BlockSpec(memory_space=pltpu.SMEM)] * 2 + [any_spec] * 6,
        out_specs=pl.BlockSpec(memory_space=pltpu.VMEM),
        scratch_shapes=[
            pltpu.VMEM((32, 128), jnp.int32), pltpu.SMEM((32, 128), jnp.int32),
            vm(na, ns, 256, 256), vm(256, 256), vm(256, 256), vm(256, 256), vm(256, 256),
            vm(nr * f1, 8, 128), vm(nr * f2, 8, 128), vm(4, nu, 8, 128), vm(4, nu, 8, 128),
            vm(2, n1, nc, 8, 128), vm(n1, 2, 2, nc, 8, 128), vm(n2, 2, 2, nc, 8, 128),
            pltpu.VMEM((n1, n1, 256, 512), BF16), pltpu.VMEM((n1, 768, 512), BF16),
            vm(nu, 2, SIDE, SIDE, 8, 256),
            vm(2, 2, nu, half, 8, 256), vm(2, 2, nu, half, 8, 256),
            vm(2, 2, nu, SIDE, 8, 256), vm(2, nu, SIDE, 8, 256),
            vm(2, nu, SIDE - 1, 8, 256),
            vm(deep, 256), vm(deep, 256), vm(deep, 256), vm(deep, 256),
            vm(nc, 2, 8, width), vm(2, nc, 8, width),
            vm(3, nc, 2, 8, 256), vm(3, nc, 8, 256), vm(3, nc, 8, 256), vm(3, nc, 8, 256),
            vm(3, 8, 256), vm(3, nz, 8, 256), vm(2, 3, 8, 256),
            dma((ns,)), dma((3,)), dma, dma, dma, dma, dma, dma,
            dma((2,)), dma((2, n1)), dma((2,)), dma((2, n1)), dma((2,)), dma((2, n1)),
            dma, dma((2, 2, nu)), dma, dma((2, 2, nu)), dma, dma((2, nu)),
            dma, dma, dma, dma((3,)), dma, dma((3,)), dma, dma((3,)), dma, dma,
        ],
        compiler_params=pltpu.CompilerParams(
            collective_id=ident, has_side_effects=True, vmem_limit_bytes=56 * 1024 * 1024
        ),
    )(struct_first, struct_second, inverse, factor_first, factor_second, link_factor, dinv_first, dinv_second)


def body(inverse, struct_first, struct_second, factor_first, factor_second, link_factor, dinv_first, dinv_second):
    na, _, ns, _, ext, _ = inverse.shape
    rows = na * 16
    args = (
        struct_first, struct_second, inverse.reshape(na, ns, ext, ext),
        factor_first, factor_second, link_factor, dinv_first, dinv_second,
    )
    roomy = lambda *v: fused(na, na, 0, *v)
    tight = lambda *v: fused(TIGHT[0], TIGHT[1], 1, *v)
    fits = pl.pallas_call(
        functools.partial(spread_fits, lax.axis_size("row")),
        out_shape=jax.ShapeDtypeStruct((1,), jnp.int32),
        in_specs=[pl.BlockSpec(memory_space=pltpu.SMEM)] * 2,
        out_specs=pl.BlockSpec(memory_space=pltpu.SMEM),
    )(struct_first, struct_second)
    o = lax.cond(fits[0] > 0, tight, roomy, *args)
    small = jax.ShapeDtypeStruct((16, 256), F32)
    tall = jax.ShapeDtypeStruct((rows, 256), F32)
    p1, p2, g1, g2, g3 = pl.pallas_call(
        functools.partial(part_out, rows),
        out_shape=(tall, tall, small, small, small),
    )(o)
    panel = lambda v: jnp.swapaxes(v.reshape(na, 1, 16, 256), 2, 3)
    turn = lambda v: jnp.swapaxes(v, 0, 1)
    return (panel(p1), turn(g1), panel(p2), turn(g2), turn(g3))


def solution(mesh):
    placed = (
        P(None, "row", None, "col", None, None),
        P(),
        P(),
        P("row", None, None),
        P("row", None, None),
        P(),
        P(),
        P(),
    )
    return jax.shard_map(
        body,
        mesh=mesh,
        in_specs=placed,
        out_specs=(
            P(None, "row", None, "col"),
            P(None, "col"),
            P(None, "row", None, "col"),
            P(None, "col"),
            P(None, "col"),
        ),
        check_vma=False,
    )
```

```python
import functools

import jax
import jax.numpy as jnp
from jax import lax
from jax.experimental import pallas as pl
from jax.experimental.pallas import tpu as pltpu
from jax.sharding import PartitionSpec as P

MESH = pl.DeviceIdType.MESH
SIDE = 4
TIGHT = (4, 3)
HAND_LAG = 3
USE_LAG = 5
F32 = jnp.float32
BF16 = jnp.bfloat16


def split(v):
    hi = v.astype(BF16)
    return hi, (v - hi.astype(F32)).astype(BF16)


def mm(p, q):
    return jnp.dot(p, q, preferred_element_type=F32)


def dot3(p, q):
    ph, plo = split(p)
    qh, qlo = split(q)
    return mm(ph, qh) + (mm(ph, qlo) + mm(plo, qh))


def kernel(
    nr, nc, na, ns, f1, f2, n1, n2, width,
    ids1, ids2, inv, fac1, fac2, link, dinv1, dinv2,
    out,
    tab_v, tab, a_v, l_v, d1_v, d2_v, lt_v,
    pf, pg, rps, rp, st, cw, lhs, w3, acc,
    hop, hopped, fb, ysum, zin, x1b, x2b, frb, grb,
    st2, rb, m_v, rx, n_v, q_v, s_v, u_v, w_v,
    ld, lds, lt, s1, pfr, pgr, rs_, rr, bs, br, zxs, zxr, cs, cr,
    r1s, r1r, r2s, fbr, zs, zr, ts, tr, es, er, qs, qr, us, ur, vs, vr,
):
    r = lax.axis_index("row")
    c = lax.axis_index("col")
    k = lax.rem(r, 2)
    z = r // 2
    nz = nr // 2
    y = c // SIDE
    x = lax.rem(c, SIDE)
    e = lax.rem(z, 2)
    mate = z * 2 + (1 - k)
    z_up = lax.rem(z + 1, nz) * 2 + k
    z_down = lax.rem(z + nz - 1, nz) * 2 + k
    lanes = pl.multiple_of(128 * e, 128)
    nu = n1 + n2
    row1, row2, rowi, rowp, rowq = 0, 8, 16, 24, 25

    def remote(src, dst, ss, rs, row, col):
        return pltpu.make_async_remote_copy(
            src_ref=src, dst_ref=dst, send_sem=ss, recv_sem=rs,
            device_id=(row, col), device_id_type=MESH,
        )

    def take(ref, sem):
        pltpu.make_async_copy(ref, ref, sem).wait()

    def load_a(b):
        return pltpu.make_async_copy(inv.at[:, b], a_v.at[:, b], ld.at[b])

    small = [
        pltpu.make_async_copy(link, l_v, lds.at[0]),
        pltpu.make_async_copy(dinv1, d1_v, lds.at[1]),
        pltpu.make_async_copy(dinv2, d2_v, lds.at[2]),
    ]
    barrier = pltpu.get_barrier_semaphore()

    def greet_row(d, carry):
        pl.semaphore_signal(barrier, inc=1, device_id=(lax.rem(r + d, nr), c), device_id_type=MESH)
        return carry

    def greet_col(d, carry):
        pl.semaphore_signal(barrier, inc=1, device_id=(r, lax.rem(c + d, nc)), device_id_type=MESH)
        return carry

    lax.fori_loop(1, nr, greet_row, 0)
    lax.fori_loop(1, nc, greet_col, 0)
    row8 = pl.multiple_of(128 * k + 8 * c, 8)
    pltpu.make_async_copy(fac1.at[:, pl.ds(row8, 8), pl.ds(lanes, 128)], pf.at[pl.ds(r * f1, f1)], pfr).start()
    pltpu.make_async_copy(fac2.at[:, pl.ds(row8, 8), pl.ds(lanes, 128)], pg.at[pl.ds(r * f2, f2)], pgr).start()
    for cp in small:
        cp.start()
    for b in range(ns):
        load_a(b).start()
    pl.semaphore_wait(barrier, nr + nc - 2)

    def send_pieces(fac, buf, count, rsem):
        def go(d, carry):
            r2 = lax.rem(r + d, nr)
            k2 = lax.rem(r2, 2)
            rows = pl.multiple_of(128 * k2 + 8 * c, 8)
            side = pl.multiple_of(128 * lax.rem(r2 // 2, 2), 128)
            remote(
                fac.at[:, pl.ds(rows, 8), pl.ds(side, 128)], buf.at[pl.ds(r * count, count)], s1, rsem, r2, c
            ).start()
            return carry

        lax.fori_loop(1, nr, go, 0)

    send_pieces(fac1, pf, f1, pfr)
    send_pieces(fac2, pg, f2, pgr)

    tile = lax.broadcasted_iota(jnp.int32, (8, 128), 1)
    at1 = jnp.zeros((8, 128), jnp.int32)
    at2 = jnp.zeros((8, 128), jnp.int32)
    for j in range(ids1.shape[0]):
        at1 = jnp.where(tile == ids1[j], j + 1, at1)
    for j in range(ids2.shape[0]):
        at2 = jnp.where(tile == ids2[j], j + 1, at2)
    in2 = jnp.where(at2 > 0, 1, 0)
    only1 = jnp.where(at1 > 0, 1, 0) - in2

    def lower(v):
        tot = jnp.zeros_like(v)
        for d in range(1, na):
            tot = tot + jnp.where(tile >= d * nc, pltpu.roll(v, d * nc, axis=1), 0)
        return tot

    def fold_tiles(v):
        tot = v
        for d in range(1, na):
            tot = tot + pltpu.roll(v, 128 - d * nc, axis=1)
        return tot

    def spread(v):
        tot = v
        for d in range(1, na):
            tot = tot + jnp.where(tile >= d * nc, pltpu.roll(v, d * nc, axis=1), 0)
        return tot

    count2 = spread(jnp.where(tile < nc, fold_tiles(in2), 0))
    rank = jnp.where(in2 > 0, lower(in2), count2 + lower(only1))
    line = lax.broadcasted_iota(jnp.int32, (8, 128), 0)
    t1 = jnp.zeros((8, 128), jnp.int32)
    t2 = jnp.zeros((8, 128), jnp.int32)
    ti = jnp.zeros((8, 128), jnp.int32)
    for a in range(n1):
        hit = jnp.logical_and(at1 > 0, rank == a)
        t1 = jnp.where(line == a, fold_tiles(jnp.where(hit, at1, 0)), t1)
        t2 = jnp.where(line == a, fold_tiles(jnp.where(hit, at2, 0)), t2)
        ti = jnp.where(line == a, fold_tiles(jnp.where(hit, tile // nc, 0)), ti)
    tab_v[0:8, :] = t1 - 1
    tab_v[8:16, :] = t2 - 1
    tab_v[16:24, :] = ti
    tab_v[24:32, :] = jnp.where(
        line == 0, jnp.where(at1 > 0, rank, -1), jnp.where(in2 > 0, rank, -1)
    )
    to_smem = pltpu.make_async_copy(tab_v, tab, lt)
    to_smem.start()
    for cp in small:
        cp.wait()
    first = jnp.where(jnp.logical_and(r == 0, c == 0), 1.0, 0.0).astype(F32)
    lt_v[...] = jnp.transpose(l_v[...])
    d1_v[...] = jnp.transpose(d1_v[...]) * first
    d2_v[...] = jnp.transpose(d2_v[...]) * first

    to_smem.wait()
    take(pf, pfr)

    def pack(fg):
        def unit(b, carry):
            u = n1 * fg + b

            def one(c2, carry2):
                j = tab[(row1, row2)[fg] + b, c2]
                v = (pf, pg)[fg][jnp.maximum(j, 0)]
                st[u, c2] = jnp.where(j >= 0, v, 0.0)
                return carry2

            lax.fori_loop(0, nc, one, 0)
            pltpu.make_async_copy(st.at[u, c], cw.at[u, e, k, c], br.at[u]).start()

            def go(d, carry2):
                c2 = lax.rem(c + d, nc)
                remote(st.at[u, c2], cw.at[u, e, k, c], bs, br.at[u], r, c2).start()
                return carry2

            lax.fori_loop(1, nc, go, 0)
            return carry

        lax.fori_loop(0, (n1, n2)[fg], unit, 0)

    pack(0)
    take(pg, pgr)
    pack(1)

    other = z + 1 - 2 * e
    for t in range(4):
        z2 = z if t < 2 else other
        k2 = k if t % 2 == 0 else 1 - k
        r2 = z2 * 2 + k2
        for a in range(n1):
            j1 = tab[row1 + a, r2]
            rps[t, a] = jnp.where(j1 >= 0, pf[jnp.maximum(j1, 0)], 0.0)
        for a in range(n2):
            j2 = tab[row2 + a, r2]
            rps[t, n1 + a] = jnp.where(j2 >= 0, pg[jnp.maximum(j2, 0)], 0.0)
        if t == 0:
            pltpu.make_async_copy(rps.at[t], rp.at[e * 2 + k], rr).start()
        else:
            remote(rps.at[t], rp.at[e * 2 + k], rs_, rr, r2, c).start()

    def ring(h):
        if h == 0:
            return x, y * SIDE + lax.rem(x + 1, SIDE), y * SIDE + lax.rem(x + SIDE - 1, SIDE)
        return y, lax.rem(y + 1, SIDE) * SIDE + x, lax.rem(y + SIDE - 1, SIDE) * SIDE + x

    half = SIDE // 2

    def part(a, h, who, lo, n):
        if h == 0:
            return acc.at[a, 0, pl.ds(lo, n), who]
        return acc.at[a, 1, who, pl.ds(lo, n)]

    def step_one(a):
        for h in range(2):
            u, right, left = ring(h)
            up, down, far = lax.rem(u + 1, SIDE), lax.rem(u + SIDE - 1, SIDE), lax.rem(u + 2, SIDE)
            remote(part(a, h, far, 0, half), hop.at[h, 0, a], r1s, r1r.at[h, 0, a], r, right).start()
            remote(part(a, h, far, half, half), hop.at[h, 1, a], r1s, r1r.at[h, 1, a], r, left).start()
            remote(
                part(a, h, up, half, half), fb.at[h, 0, a, pl.ds(half, half)], r1s, fbr.at[h, 0, a], r, right
            ).start()
            remote(
                part(a, h, down, 0, half), fb.at[h, 1, a, pl.ds(0, half)], r1s, fbr.at[h, 1, a], r, left
            ).start()

    def weights(u):
        ff = jnp.concatenate([cw[u, 0].reshape(256, 128), cw[u, 1].reshape(256, 128)], axis=1)
        fh, fl = split(ff)
        w3[u, 0:256] = fh
        w3[u, 256:512] = fl
        w3[u, 512:768] = fh

    def term(fg, a, b):
        v = lhs[b, a]
        return mm(jnp.concatenate([v[:, 0:256], v[:, 0:256], v[:, 256:512]], axis=1), w3[n1 * fg + b])

    def shaped(v):
        return v.reshape(2, SIDE, SIDE, 8, 256)

    def part_sums(fg, b):
        def one(a, carry):
            u = n1 * fg + a
            got = shaped(term(fg, a, b))
            if fg == 1:
                acc[u] += got
            else:

                @pl.when(b == 0)
                def _():
                    acc[u] = got

                @pl.when(b > 0)
                def _():
                    acc[u] += got

            return carry

        lax.fori_loop(0, (n1, n2)[fg], one, 0)

    def finish(fg):
        n = (n1, n2)[fg]

        def one(a, carry):
            u = n1 * fg + a
            acc[u] += shaped(term(fg, a, n - 2) + term(fg, a, n - 1))
            step_one(u)
            return carry

        lax.fori_loop(0, n, one, 0)

    def start_second(a, carry):
        acc[n1 + a] = shaped(-dot3(acc[a].reshape(256, 256), l_v[...]))
        return carry

    def swap(u):
        mine = cw.at[u, e, k]
        take(mine, br.at[u])
        remote(mine, mine, cs, cr.at[u], mate, c).start()
        remote(mine, mine, zxs, zxr.at[u], jnp.where(lax.rem(u, 2) == 0, z_down, z_up), c).start()

    def hand(u):
        got = cw.at[u, 1 - e, k]
        take(got, zxr.at[u])
        remote(got, got, cs, cr.at[u], mate, c).start()

    def units(s, carry):
        @pl.when(s < nu)
        def _():
            swap(s)

        @pl.when(jnp.logical_and(s >= HAND_LAG, s < nu + HAND_LAG))
        def _():
            hand(s - HAND_LAG)

        @pl.when(s >= USE_LAG)
        def _():
            u = s - USE_LAG
            take(cw.at[u, :, 1 - k], cr.at[u])
            weights(u)

            @pl.when(u < n1 - 2)
            def _():
                part_sums(0, u)

            @pl.when(u == n1 - 1)
            def _():
                finish(0)
                lax.fori_loop(0, n2, start_second, 0)

            @pl.when(jnp.logical_and(u >= n1, u < nu - 2))
            def _():
                part_sums(1, u - n1)

            @pl.when(u == nu - 1)
            def _():
                finish(1)

        return carry

    for b in range(ns):
        load_a(b).wait()

    def cast(i, carry):
        a, b = i // n1, lax.rem(i, n1)
        ah, al = split(a_v[tab[rowi + a, r], tab[rowi + b, c]])
        lhs[b, a, :, 0:256] = ah
        lhs[b, a, :, 256:512] = al
        return carry

    lax.fori_loop(0, n1 * n1, cast, 0)
    lax.fori_loop(0, nu + USE_LAG, units, 0)

    def step_two(a, carry):
        for h in range(2):
            u, right, left = ring(h)
            up, down = lax.rem(u + 1, SIDE), lax.rem(u + SIDE - 1, SIDE)
            take(hop.at[h, 0, a], r1r.at[h, 0, a])
            hopped[h, 0, a] = hop[h, 0, a] + part(a, h, up, 0, half)[...]
            remote(
                hopped.at[h, 0, a], fb.at[h, 0, a, pl.ds(0, half)], r2s, fbr.at[h, 0, a], r, right
            ).start()
            take(hop.at[h, 1, a], r1r.at[h, 1, a])
            hopped[h, 1, a] = hop[h, 1, a] + part(a, h, down, half, half)[...]
            remote(
                hopped.at[h, 1, a], fb.at[h, 1, a, pl.ds(half, half)], r2s, fbr.at[h, 1, a], r, left
            ).start()
        return carry

    lax.fori_loop(0, nu, step_two, 0)

    take(rp, rr)
    frb[...] = jnp.zeros_like(frb)
    grb[...] = jnp.zeros_like(grb)
    x1b[...] = jnp.zeros_like(x1b)
    x2b[...] = jnp.zeros_like(x2b)
    for h in range(2):
        for g in range(2):
            for a in range(n1):
                frb[a * 16 + h * 8:a * 16 + h * 8 + 8, g * 128:g * 128 + 128] = rp[g * 2 + h, a]
            for a in range(n2):
                grb[a * 16 + h * 8:a * 16 + h * 8 + 8, g * 128:g * 128 + 128] = rp[g * 2 + h, n1 + a]

    def second(a, carry):
        for h in range(2):
            u = ring(h)[0]
            take(fb.at[h, 0, a], fbr.at[h, 0, a])
            take(fb.at[h, 1, a], fbr.at[h, 1, a])
            ysum[h, a] = part(a, h, u, 0, SIDE)[...] + (fb[h, 0, a] + fb[h, 1, a])
            v = y if h == 0 else x
            for d in range(1, SIDE):
                v2 = lax.rem(v + d, SIDE)
                col = v2 * SIDE + x if h == 0 else y * SIDE + v2
                remote(ysum.at[h, a, v2], zin.at[h, a, d - 1], zs, zr.at[h, a], r, col).start()
        return carry

    lax.fori_loop(0, nu, second, 0)

    def gather(fg, buf):
        def one(a, carry):
            u = n1 * fg + a
            for h in range(2):
                v = y if h == 0 else x
                take(zin.at[h, u], zr.at[h, u])
                tot = ysum[h, u, v] + (zin[h, u, 0] + zin[h, u, 1] + zin[h, u, 2])
                buf[pl.ds(pl.multiple_of(a * 16 + h * 8, 8), 8), :] = tot
            return carry

        lax.fori_loop(0, (n1, n2)[fg], one, 0)

    gather(0, x1b)
    x1 = x1b[...]
    d1t = dot3(jnp.transpose(x1), frb[...]) + d1_v[...]
    m_v[0] = d1t.reshape(nc, 2, 8, 256)
    jt = dot3(lt_v[...], d1t) - dot3(jnp.transpose(grb[...]), x1)
    m_v[1] = jt.reshape(nc, 2, 8, 256)

    def fold(t):
        return remote(m_v.at[t, :, 1 - k], rx.at[t], es, er.at[t], mate, c)

    fold(0).start()
    fold(1).start()
    base = dot3(jt, l_v[...]) + d2_v[...]
    gather(1, x2b)
    et = dot3(jnp.transpose(x2b[...]), grb[...]) + base
    m_v[2] = et.reshape(nc, 2, 8, 256)
    fold(2).start()

    def send_term(t):
        take(rx.at[t], er.at[t])
        n_v[t] = m_v[t, :, k] + rx[t]
        pltpu.make_async_copy(n_v.at[t, c], q_v.at[t, c], qr.at[t]).start()

        def go(d, carry):
            c2 = lax.rem(c + d, nc)
            remote(n_v.at[t, c2], q_v.at[t, c], qs, qr.at[t], r, c2).start()
            return carry

        lax.fori_loop(1, nc, go, 0)

    for t in range(3):
        send_term(t)

    lane = lax.broadcasted_iota(jnp.int32, (16, 128), 1) // 16
    for c2 in range(nc):
        blk, off = c2 // 8, c2 % 8
        for q in range(width // 128):
            val = jnp.zeros((16, 128), F32)
            for g in range(8):
                u = q * 8 + g
                if u < nu:
                    buf, a = (x1b, u) if u < n1 else (x2b, u - n1)
                    src = buf[a * 16:a * 16 + 16, blk * 128:blk * 128 + 128]
                    shift = (16 * (g - off)) % 128
                    if shift:
                        src = pltpu.roll(src, shift, axis=1)
                    val = jnp.where(lane == g, src, val)
            st2[c2, :, :, q * 128:(q + 1) * 128] = val.reshape(2, 8, 128)
    pltpu.make_async_copy(st2.at[c], rb.at[:, c], tr).start()

    def send_cols(d, carry):
        c2 = lax.rem(c + d, nc)
        remote(st2.at[c2], rb.at[:, c], ts, tr, r, c2).start()
        return carry

    lax.fori_loop(1, nc, send_cols, 0)

    def send_sum(t):
        take(q_v.at[t], qr.at[t])
        tot = q_v[t, 0]
        for i in range(1, nc):
            tot = tot + q_v[t, i]
        s_v[t] = tot
        pltpu.make_async_copy(s_v.at[t], u_v.at[t, z], ur.at[t]).start()

        def go(d, carry):
            z2 = lax.rem(z + d, nz)
            remote(s_v.at[t], u_v.at[t, z], us, ur.at[t], z2 * 2 + k, c).start()
            return carry

        lax.fori_loop(1, nz, go, 0)

    for t in range(3):
        send_sum(t)

    take(rb, tr)
    cols = jnp.transpose(rb[...].reshape(256, width))
    for fg in range(2):
        for a in range(na):
            slot_of = tab[(rowp, rowq)[fg], a * nr + r]
            val = jnp.zeros((16, 256), F32)
            for i in range((n1, n2)[fg]):
                lo = (n1 * fg + i) * 16
                val = jnp.where(slot_of == i, -cols[lo:lo + 16, :], val)
            lo = (na * fg + a) * 16
            out[lo:lo + 16, :] = val

    for t in range(3):
        take(u_v.at[t], ur.at[t])
        tot = u_v[t, 0]
        for i in range(1, nz):
            tot = tot + u_v[t, i]
        w_v[k, t] = tot
    last = remote(w_v.at[k], w_v.at[k], vs, vr, mate, c)
    last.start()
    take(w_v.at[k], vr)
    for h in range(2):
        lo = na * 32 + h * 8
        out[lo:lo + 8, :] = w_v[h, 0]
        out[lo + 16:lo + 24, :] = -w_v[h, 1]
        out[lo + 32:lo + 40, :] = w_v[h, 2]

    take(pf.at[pl.ds(0, (nr - 1) * f1)], s1)
    take(pg.at[pl.ds(0, (nr - 1) * f2)], s1)
    take(st.at[:, pl.ds(0, nc - 1)], bs)
    take(cw.at[:, :, 0], cs)
    take(cw.at[:, 0, 0], zxs)
    take(rp.at[pl.ds(0, 3)], rs_)
    take(fb, r1s)
    take(hop, r2s)
    take(zin, zs)
    take(rb.at[:, pl.ds(0, nc - 1)], ts)
    take(rx, es)
    take(q_v.at[:, pl.ds(0, nc - 1)], qs)
    take(u_v.at[:, pl.ds(0, nz - 1)], us)
    take(w_v.at[0], vs)


def spread_fits(n, ids1, ids2, out):
    lane = lax.broadcasted_iota(jnp.int32, (8, 128), 1)
    bad = jnp.zeros((8, 128), F32)
    for ids, most in ((ids1, TIGHT[0]), (ids2, TIGHT[1])):
        count = jnp.zeros((8, 128), F32)
        for j in range(ids.shape[0]):
            count = count + jnp.where(lane == lax.rem(ids[j], n), 1.0, 0.0)
        bad = jnp.maximum(bad, count - most)
    out[0] = jnp.where(jnp.max(bad) > 0.5, 0, 1)


def part_out(rows, o, p1, p2, g1, g2, g3):
    p1[...] = o[0:rows, :]
    p2[...] = o[rows:2 * rows, :]
    for n, g in enumerate((g1, g2, g3)):
        g[...] = o[2 * rows + 16 * n:2 * rows + 16 * n + 16, :]


def fused(n1, n2, ident, struct_first, struct_second, inverse, factor_first, factor_second, link_factor, dinv_first, dinv_second):
    nr = lax.axis_size("row")
    nc = lax.axis_size("col")
    na, ns, ext, _ = inverse.shape
    f1, f2 = factor_first.shape[0], factor_second.shape[0]
    assert nr == nc == SIDE * SIDE and na == ns and na * nc <= 128 and n1 <= 8
    nu = n1 + n2
    nz = nr // 2
    width = -(-nu * 16 // 128) * 128
    deep = -(-n1 * 16 // 128) * 128
    rows = na * 16
    any_spec = pl.BlockSpec(memory_space=pl.ANY)
    vm = lambda *s: pltpu.VMEM(s, F32)
    dma = pltpu.SemaphoreType.DMA
    half = SIDE // 2
    return pl.pallas_call(
        functools.partial(kernel, nr, nc, na, ns, f1, f2, n1, n2, width),
        out_shape=jax.ShapeDtypeStruct((2 * rows + 48, 256), F32),
        in_specs=[pl.BlockSpec(memory_space=pltpu.SMEM)] * 2 + [any_spec] * 6,
        out_specs=pl.BlockSpec(memory_space=pltpu.VMEM),
        scratch_shapes=[
            pltpu.VMEM((32, 128), jnp.int32), pltpu.SMEM((32, 128), jnp.int32),
            vm(na, ns, 256, 256), vm(256, 256), vm(256, 256), vm(256, 256), vm(256, 256),
            vm(nr * f1, 8, 128), vm(nr * f2, 8, 128), vm(4, nu, 8, 128), vm(4, nu, 8, 128),
            vm(nu, nc, 8, 128), vm(nu, 2, 2, nc, 8, 128),
            pltpu.VMEM((n1, n1, 256, 512), BF16), pltpu.VMEM((nu, 768, 256), BF16),
            vm(nu, 2, SIDE, SIDE, 8, 256),
            vm(2, 2, nu, half, 8, 256), vm(2, 2, nu, half, 8, 256),
            vm(2, 2, nu, SIDE, 8, 256), vm(2, nu, SIDE, 8, 256),
            vm(2, nu, SIDE - 1, 8, 256),
            vm(deep, 256), vm(deep, 256), vm(deep, 256), vm(deep, 256),
            vm(nc, 2, 8, width), vm(2, nc, 8, width),
            vm(3, nc, 2, 8, 256), vm(3, nc, 8, 256), vm(3, nc, 8, 256), vm(3, nc, 8, 256),
            vm(3, 8, 256), vm(3, nz, 8, 256), vm(2, 3, 8, 256),
            dma((ns,)), dma((3,)), dma, dma, dma, dma, dma, dma,
            dma, dma((nu,)), dma, dma((nu,)), dma, dma((nu,)),
            dma, dma((2, 2, nu)), dma, dma((2, 2, nu)), dma, dma((2, nu)),
            dma, dma, dma, dma((3,)), dma, dma((3,)), dma, dma((3,)), dma, dma,
        ],
        compiler_params=pltpu.CompilerParams(
            collective_id=ident, has_side_effects=True, vmem_limit_bytes=56 * 1024 * 1024
        ),
    )(struct_first, struct_second, inverse, factor_first, factor_second, link_factor, dinv_first, dinv_second)


def body(inverse, struct_first, struct_second, factor_first, factor_second, link_factor, dinv_first, dinv_second):
    na, _, ns, _, ext, _ = inverse.shape
    rows = na * 16
    args = (
        struct_first, struct_second, inverse.reshape(na, ns, ext, ext),
        factor_first, factor_second, link_factor, dinv_first, dinv_second,
    )
    roomy = lambda *v: fused(na, na, 0, *v)
    tight = lambda *v: fused(TIGHT[0], TIGHT[1], 1, *v)
    fits = pl.pallas_call(
        functools.partial(spread_fits, lax.axis_size("row")),
        out_shape=jax.ShapeDtypeStruct((1,), jnp.int32),
        in_specs=[pl.BlockSpec(memory_space=pltpu.SMEM)] * 2,
        out_specs=pl.BlockSpec(memory_space=pltpu.SMEM),
    )(struct_first, struct_second)
    o = lax.cond(fits[0] > 0, tight, roomy, *args)
    small = jax.ShapeDtypeStruct((16, 256), F32)
    tall = jax.ShapeDtypeStruct((rows, 256), F32)
    p1, p2, g1, g2, g3 = pl.pallas_call(
        functools.partial(part_out, rows),
        out_shape=(tall, tall, small, small, small),
    )(o)
    panel = lambda v: jnp.swapaxes(v.reshape(na, 1, 16, 256), 2, 3)
    turn = lambda v: jnp.swapaxes(v, 0, 1)
    return (panel(p1), turn(g1), panel(p2), turn(g2), turn(g3))


def solution(mesh):
    placed = (
        P(None, "row", None, "col", None, None),
        P(),
        P(),
        P("row", None, None),
        P("row", None, None),
        P(),
        P(),
        P(),
    )
    return jax.shard_map(
        body,
        mesh=mesh,
        in_specs=placed,
        out_specs=(
            P(None, "row", None, "col"),
            P(None, "col"),
            P(None, "row", None, "col"),
            P(None, "col"),
            P(None, "col"),
        ),
        check_vma=False,
    )
```

```python
import functools

import jax
import jax.numpy as jnp
from jax import lax
from jax.experimental import pallas as pl
from jax.experimental.pallas import tpu as pltpu
from jax.sharding import PartitionSpec as P

MESH = pl.DeviceIdType.MESH
SIDE = 4
TIGHT = (4, 3)
HAND_LAG = 3
USE_LAG = 5
F32 = jnp.float32
BF16 = jnp.bfloat16


def split(v):
    hi = v.astype(BF16)
    return hi, (v - hi.astype(F32)).astype(BF16)


def mm(p, q):
    return jnp.dot(p, q, preferred_element_type=F32)


def dot3(p, q):
    ph, plo = split(p)
    qh, qlo = split(q)
    return mm(ph, qh) + (mm(ph, qlo) + mm(plo, qh))


def kernel(
    nr, nc, na, ns, f1, f2, n1, n2, width,
    ids1, ids2, inv, fac1, fac2, link, dinv1, dinv2,
    out,
    tab_v, tab, a_v, l_v, d1_v, d2_v, lt_v,
    pf, pg, rps, rp, st, cw, lhs, w3, acc,
    hop, hopped, fb, ysum, zin, x1b, x2b, wq,
    st2, rb, m_v, rx, n_v, q_v, s_v, u_v, w_v,
    ld, lds, lt, s1, pfr, pgr, rs_, rr, bs, br, zxs, zxr, cs, cr,
    r1s, r1r, r2s, fbr, zs, zr, ws, wr, ts, tr, es, er, qs, qr, us, ur, vs, vr,
):
    r = lax.axis_index("row")
    c = lax.axis_index("col")
    k = lax.rem(r, 2)
    z = r // 2
    nz = nr // 2
    y = c // SIDE
    x = lax.rem(c, SIDE)
    e = lax.rem(z, 2)
    mate = z * 2 + (1 - k)
    z_up = lax.rem(z + 1, nz) * 2 + k
    z_down = lax.rem(z + nz - 1, nz) * 2 + k
    lanes = pl.multiple_of(128 * e, 128)
    nu = n1 + n2
    row1, row2, rowi, rowp, rowq = 0, 8, 16, 24, 25

    def remote(src, dst, ss, rs, row, col):
        return pltpu.make_async_remote_copy(
            src_ref=src, dst_ref=dst, send_sem=ss, recv_sem=rs,
            device_id=(row, col), device_id_type=MESH,
        )

    def row_at(i):
        step = (i + 1) // 2
        return lax.rem(r + nr // 2 + jnp.where(lax.rem(i, 2) == 1, step, -step), nr)

    def z_at(i):
        step = (i + 1) // 2
        return lax.rem(z + nz // 2 + jnp.where(lax.rem(i, 2) == 1, step, -step), nz)

    plane = sorted(
        ((dy, dx) for dy in range(SIDE) for dx in range(SIDE) if dy or dx),
        key=lambda v: -(min(v[0], SIDE - v[0]) + min(v[1], SIDE - v[1])),
    )

    def plane_cols():
        return [lax.rem(y + dy, SIDE) * SIDE + lax.rem(x + dx, SIDE) for dy, dx in plane]

    def take(ref, sem):
        pltpu.make_async_copy(ref, ref, sem).wait()

    def load_a(b):
        return pltpu.make_async_copy(inv.at[:, b], a_v.at[:, b], ld.at[b])

    small = [
        pltpu.make_async_copy(link, l_v, lds.at[0]),
        pltpu.make_async_copy(dinv1, d1_v, lds.at[1]),
        pltpu.make_async_copy(dinv2, d2_v, lds.at[2]),
    ]
    barrier = pltpu.get_barrier_semaphore()

    def greet_row(d, carry):
        pl.semaphore_signal(barrier, inc=1, device_id=(lax.rem(r + d, nr), c), device_id_type=MESH)
        return carry

    def greet_col(d, carry):
        pl.semaphore_signal(barrier, inc=1, device_id=(r, lax.rem(c + d, nc)), device_id_type=MESH)
        return carry

    lax.fori_loop(1, nr, greet_row, 0)
    lax.fori_loop(1, nc, greet_col, 0)
    row8 = pl.multiple_of(128 * k + 8 * c, 8)
    pltpu.make_async_copy(fac1.at[:, pl.ds(row8, 8), pl.ds(lanes, 128)], pf.at[pl.ds(r * f1, f1)], pfr).start()
    pltpu.make_async_copy(fac2.at[:, pl.ds(row8, 8), pl.ds(lanes, 128)], pg.at[pl.ds(r * f2, f2)], pgr).start()
    for cp in small:
        cp.start()
    for b in range(ns):
        load_a(b).start()
    pl.semaphore_wait(barrier, nr + nc - 2)

    def send_pieces(fac, buf, count, rsem):
        def go(d, carry):
            r2 = row_at(d)
            k2 = lax.rem(r2, 2)
            rows = pl.multiple_of(128 * k2 + 8 * c, 8)
            side = pl.multiple_of(128 * lax.rem(r2 // 2, 2), 128)
            remote(
                fac.at[:, pl.ds(rows, 8), pl.ds(side, 128)], buf.at[pl.ds(r * count, count)], s1, rsem, r2, c
            ).start()
            return carry

        lax.fori_loop(0, nr - 1, go, 0)

    send_pieces(fac1, pf, f1, pfr)
    send_pieces(fac2, pg, f2, pgr)

    tile = lax.broadcasted_iota(jnp.int32, (8, 128), 1)
    at1 = jnp.zeros((8, 128), jnp.int32)
    at2 = jnp.zeros((8, 128), jnp.int32)
    for j in range(ids1.shape[0]):
        at1 = jnp.where(tile == ids1[j], j + 1, at1)
    for j in range(ids2.shape[0]):
        at2 = jnp.where(tile == ids2[j], j + 1, at2)
    in2 = jnp.where(at2 > 0, 1, 0)
    only1 = jnp.where(at1 > 0, 1, 0) - in2

    def lower(v):
        tot = jnp.zeros_like(v)
        for d in range(1, na):
            tot = tot + jnp.where(tile >= d * nc, pltpu.roll(v, d * nc, axis=1), 0)
        return tot

    def fold_tiles(v):
        tot = v
        for d in range(1, na):
            tot = tot + pltpu.roll(v, 128 - d * nc, axis=1)
        return tot

    def spread(v):
        tot = v
        for d in range(1, na):
            tot = tot + jnp.where(tile >= d * nc, pltpu.roll(v, d * nc, axis=1), 0)
        return tot

    count2 = spread(jnp.where(tile < nc, fold_tiles(in2), 0))
    rank = jnp.where(in2 > 0, lower(in2), count2 + lower(only1))
    line = lax.broadcasted_iota(jnp.int32, (8, 128), 0)
    t1 = jnp.zeros((8, 128), jnp.int32)
    t2 = jnp.zeros((8, 128), jnp.int32)
    ti = jnp.zeros((8, 128), jnp.int32)
    for a in range(n1):
        hit = jnp.logical_and(at1 > 0, rank == a)
        t1 = jnp.where(line == a, fold_tiles(jnp.where(hit, at1, 0)), t1)
        t2 = jnp.where(line == a, fold_tiles(jnp.where(hit, at2, 0)), t2)
        ti = jnp.where(line == a, fold_tiles(jnp.where(hit, tile // nc, 0)), ti)
    tab_v[0:8, :] = t1 - 1
    tab_v[8:16, :] = t2 - 1
    tab_v[16:24, :] = ti
    tab_v[24:32, :] = jnp.where(
        line == 0, jnp.where(at1 > 0, rank, -1), jnp.where(in2 > 0, rank, -1)
    )
    to_smem = pltpu.make_async_copy(tab_v, tab, lt)
    to_smem.start()
    for cp in small:
        cp.wait()
    first = jnp.where(jnp.logical_and(r == 0, c == 0), 1.0, 0.0).astype(F32)
    lt_v[...] = jnp.transpose(l_v[...])
    d1_v[...] = jnp.transpose(d1_v[...]) * first
    d2_v[...] = jnp.transpose(d2_v[...]) * first

    to_smem.wait()
    take(pf, pfr)

    def pack(fg):
        def unit(b, carry):
            u = n1 * fg + b

            def one(c2, carry2):
                j = tab[(row1, row2)[fg] + b, c2]
                v = (pf, pg)[fg][jnp.maximum(j, 0)]
                st[u, c2] = jnp.where(j >= 0, v, 0.0)
                return carry2

            lax.fori_loop(0, nc, one, 0)
            pltpu.make_async_copy(st.at[u, c], cw.at[u, e, k, c], br.at[u]).start()

            for c2 in plane_cols():
                remote(st.at[u, c2], cw.at[u, e, k, c], bs, br.at[u], r, c2).start()
            return carry

        lax.fori_loop(0, (n1, n2)[fg], unit, 0)

    pack(0)
    take(pg, pgr)
    pack(1)

    other = z + 1 - 2 * e
    for t in range(4):
        z2 = z if t < 2 else other
        k2 = k if t % 2 == 0 else 1 - k
        r2 = z2 * 2 + k2
        for a in range(n1):
            j1 = tab[row1 + a, r2]
            rps[t, a] = jnp.where(j1 >= 0, pf[jnp.maximum(j1, 0)], 0.0)
        for a in range(n2):
            j2 = tab[row2 + a, r2]
            rps[t, n1 + a] = jnp.where(j2 >= 0, pg[jnp.maximum(j2, 0)], 0.0)
        if t == 0:
            pltpu.make_async_copy(rps.at[t], rp.at[e * 2 + k], rr).start()
        else:
            remote(rps.at[t], rp.at[e * 2 + k], rs_, rr, r2, c).start()

    def ring(h):
        if h == 0:
            return x, y * SIDE + lax.rem(x + 1, SIDE), y * SIDE + lax.rem(x + SIDE - 1, SIDE)
        return y, lax.rem(y + 1, SIDE) * SIDE + x, lax.rem(y + SIDE - 1, SIDE) * SIDE + x

    half = SIDE // 2

    def part(a, h, who, lo, n):
        if h == 0:
            return acc.at[a, 0, pl.ds(lo, n), who]
        return acc.at[a, 1, who, pl.ds(lo, n)]

    def step_one(a):
        for h in range(2):
            u, right, left = ring(h)
            up, down, far = lax.rem(u + 1, SIDE), lax.rem(u + SIDE - 1, SIDE), lax.rem(u + 2, SIDE)
            remote(part(a, h, far, 0, half), hop.at[h, 0, a], r1s, r1r.at[h, 0, a], r, right).start()
            remote(part(a, h, far, half, half), hop.at[h, 1, a], r1s, r1r.at[h, 1, a], r, left).start()
            remote(
                part(a, h, up, half, half), fb.at[h, 0, a, pl.ds(half, half)], r1s, fbr.at[h, 0, a], r, right
            ).start()
            remote(
                part(a, h, down, 0, half), fb.at[h, 1, a, pl.ds(0, half)], r1s, fbr.at[h, 1, a], r, left
            ).start()

    def weights(u):
        ff = jnp.concatenate([cw[u, 0].reshape(256, 128), cw[u, 1].reshape(256, 128)], axis=1)
        fh, fl = split(ff)
        w3[u, 0:256] = fh
        w3[u, 256:512] = fl
        w3[u, 512:768] = fh

    def term(fg, a, b):
        v = lhs[b, a]
        return mm(jnp.concatenate([v[:, 0:256], v[:, 0:256], v[:, 256:512]], axis=1), w3[n1 * fg + b])

    def shaped(v):
        return v.reshape(2, SIDE, SIDE, 8, 256)

    def part_sums(fg, b):
        def one(a, carry):
            u = n1 * fg + a
            got = shaped(term(fg, a, b))
            if fg == 1:
                acc[u] += got
            else:

                @pl.when(b == 0)
                def _():
                    acc[u] = got

                @pl.when(b > 0)
                def _():
                    acc[u] += got

            return carry

        lax.fori_loop(0, (n1, n2)[fg], one, 0)

    def finish(fg):
        n = (n1, n2)[fg]

        def one(a, carry):
            u = n1 * fg + a
            acc[u] += shaped(term(fg, a, n - 2) + term(fg, a, n - 1))
            step_one(u)
            return carry

        lax.fori_loop(0, n, one, 0)

    def start_second(a, carry):
        acc[n1 + a] = shaped(-dot3(acc[a].reshape(256, 256), l_v[...]))
        return carry

    def row_pieces():
        take(rp, rr)
        for h in range(2):
            v = y if h == 0 else x
            for u in range(nu):
                for g in range(2):
                    wq[h, u, v, :, g * 128:g * 128 + 128] = rp[g * 2 + h, u]
            for d in range(1, SIDE):
                v2 = lax.rem(v + d, SIDE)
                col = v2 * SIDE + x if h == 0 else y * SIDE + v2
                remote(wq.at[h, :, v], wq.at[h, :, v], ws, wr, r, col).start()

    def swap(u):
        mine = cw.at[u, e, k]
        take(mine, br.at[u])
        remote(mine, mine, cs, cr.at[u], mate, c).start()
        remote(mine, mine, zxs, zxr.at[u], jnp.where(lax.rem(u, 2) == 0, z_down, z_up), c).start()

    def hand(u):
        got = cw.at[u, 1 - e, k]
        take(got, zxr.at[u])
        remote(got, got, cs, cr.at[u], mate, c).start()

    def units(s, carry):
        @pl.when(s < nu)
        def _():
            swap(s)

        @pl.when(jnp.logical_and(s >= HAND_LAG, s < nu + HAND_LAG))
        def _():
            hand(s - HAND_LAG)

        @pl.when(s == USE_LAG - 1)
        def _():
            row_pieces()

        @pl.when(s >= USE_LAG)
        def _():
            u = s - USE_LAG
            take(cw.at[u, :, 1 - k], cr.at[u])
            weights(u)

            @pl.when(u < n1 - 2)
            def _():
                part_sums(0, u)

            @pl.when(u == n1 - 1)
            def _():
                finish(0)
                lax.fori_loop(0, n2, start_second, 0)

            @pl.when(jnp.logical_and(u >= n1, u < nu - 2))
            def _():
                part_sums(1, u - n1)

            @pl.when(u == nu - 1)
            def _():
                finish(1)

        return carry

    for b in range(ns):
        load_a(b).wait()

    def cast(i, carry):
        a, b = i // n1, lax.rem(i, n1)
        ah, al = split(a_v[tab[rowi + a, r], tab[rowi + b, c]])
        lhs[b, a, :, 0:256] = ah
        lhs[b, a, :, 256:512] = al
        return carry

    lax.fori_loop(0, n1 * n1, cast, 0)
    lax.fori_loop(0, nu + USE_LAG, units, 0)

    def step_two(a, carry):
        for h in range(2):
            u, right, left = ring(h)
            up, down = lax.rem(u + 1, SIDE), lax.rem(u + SIDE - 1, SIDE)
            take(hop.at[h, 0, a], r1r.at[h, 0, a])
            hopped[h, 0, a] = hop[h, 0, a] + part(a, h, up, 0, half)[...]
            remote(
                hopped.at[h, 0, a], fb.at[h, 0, a, pl.ds(0, half)], r2s, fbr.at[h, 0, a], r, right
            ).start()
            take(hop.at[h, 1, a], r1r.at[h, 1, a])
            hopped[h, 1, a] = hop[h, 1, a] + part(a, h, down, half, half)[...]
            remote(
                hopped.at[h, 1, a], fb.at[h, 1, a, pl.ds(half, half)], r2s, fbr.at[h, 1, a], r, left
            ).start()
        return carry

    lax.fori_loop(0, nu, step_two, 0)

    def second(a, carry):
        for h in range(2):
            u = ring(h)[0]
            take(fb.at[h, 0, a], fbr.at[h, 0, a])
            take(fb.at[h, 1, a], fbr.at[h, 1, a])
            ysum[h, a] = part(a, h, u, 0, SIDE)[...] + (fb[h, 0, a] + fb[h, 1, a])
            v = y if h == 0 else x
            for d in range(1, SIDE):
                v2 = lax.rem(v + d, SIDE)
                col = v2 * SIDE + x if h == 0 else y * SIDE + v2
                remote(ysum.at[h, a, v2], zin.at[h, a, d - 1], zs, zr.at[h, a], r, col).start()
        return carry


    def gather(fg, buf):
        def one(a, carry):
            u = n1 * fg + a
            for h in range(2):
                v = y if h == 0 else x
                take(zin.at[h, u], zr.at[h, u])
                tot = ysum[h, u, v] + (zin[h, u, 0] + zin[h, u, 1] + zin[h, u, 2])
                buf[pl.ds(pl.multiple_of(a * 16 + h * 8, 8), 8), :] = tot
            return carry

        lax.fori_loop(0, (n1, n2)[fg], one, 0)

    def terms(fg):
        lo, n = ((0, n1), (n1, n2))[fg]
        return ysum[:, lo:lo + n].reshape(2 * n * SIDE * 8, 256)

    def own_rows(fg):
        lo, n = ((0, n1), (n1, n2))[fg]
        return wq[:, lo:lo + n].reshape(2 * n * SIDE * 8, 256)

    lax.fori_loop(0, n1, second, 0)
    take(wq.at[:, :, pl.ds(0, SIDE - 1)], wr)
    d1t = dot3(jnp.transpose(terms(0)), own_rows(0)) + d1_v[...]
    m_v[0] = d1t.reshape(nc, 2, 8, 256)
    common = ysum[:, 0:n2].reshape(2 * n2 * SIDE * 8, 256)
    jt = dot3(lt_v[...], d1t) - dot3(jnp.transpose(own_rows(1)), common)
    m_v[1] = jt.reshape(nc, 2, 8, 256)

    def fold(t):
        return remote(m_v.at[t, :, 1 - k], rx.at[t], es, er.at[t], mate, c)

    fold(0).start()
    fold(1).start()
    base = dot3(jt, l_v[...]) + d2_v[...]
    lax.fori_loop(n1, nu, second, 0)
    et = dot3(jnp.transpose(terms(1)), own_rows(1)) + base
    m_v[2] = et.reshape(nc, 2, 8, 256)
    fold(2).start()

    def send_term(t):
        take(rx.at[t], er.at[t])
        n_v[t] = m_v[t, :, k] + rx[t]
        pltpu.make_async_copy(n_v.at[t, c], q_v.at[t, c], qr.at[t]).start()

        for c2 in plane_cols():
            remote(n_v.at[t, c2], q_v.at[t, c], qs, qr.at[t], r, c2).start()

    for t in range(3):
        send_term(t)

    gather(0, x1b)
    gather(1, x2b)

    lane = lax.broadcasted_iota(jnp.int32, (16, 128), 1) // 16
    for c2 in range(nc):
        blk, off = c2 // 8, c2 % 8
        for q in range(width // 128):
            val = jnp.zeros((16, 128), F32)
            for g in range(8):
                u = q * 8 + g
                if u < nu:
                    buf, a = (x1b, u) if u < n1 else (x2b, u - n1)
                    src = buf[a * 16:a * 16 + 16, blk * 128:blk * 128 + 128]
                    shift = (16 * (g - off)) % 128
                    if shift:
                        src = pltpu.roll(src, shift, axis=1)
                    val = jnp.where(lane == g, src, val)
            st2[c2, :, :, q * 128:(q + 1) * 128] = val.reshape(2, 8, 128)
    pltpu.make_async_copy(st2.at[c], rb.at[:, c], tr).start()

    def send_cols(d, carry):
        c2 = lax.rem(c + d, nc)
        remote(st2.at[c2], rb.at[:, c], ts, tr, r, c2).start()
        return carry

    lax.fori_loop(1, nc, send_cols, 0)

    def send_sum(t):
        take(q_v.at[t], qr.at[t])
        tot = q_v[t, 0]
        for i in range(1, nc):
            tot = tot + q_v[t, i]
        s_v[t] = tot
        pltpu.make_async_copy(s_v.at[t], u_v.at[t, z], ur.at[t]).start()

        def go(d, carry):
            z2 = z_at(d)
            remote(s_v.at[t], u_v.at[t, z], us, ur.at[t], z2 * 2 + k, c).start()
            return carry

        lax.fori_loop(0, nz - 1, go, 0)

    for t in range(3):
        send_sum(t)

    take(rb, tr)
    cols = jnp.transpose(rb[...].reshape(256, width))
    for fg in range(2):
        for a in range(na):
            slot_of = tab[(rowp, rowq)[fg], a * nr + r]
            val = jnp.zeros((16, 256), F32)
            for i in range((n1, n2)[fg]):
                lo = (n1 * fg + i) * 16
                val = jnp.where(slot_of == i, -cols[lo:lo + 16, :], val)
            lo = (na * fg + a) * 16
            out[lo:lo + 16, :] = val

    for t in range(3):
        take(u_v.at[t], ur.at[t])
        tot = u_v[t, 0]
        for i in range(1, nz):
            tot = tot + u_v[t, i]
        w_v[k, t] = tot
    last = remote(w_v.at[k], w_v.at[k], vs, vr, mate, c)
    last.start()
    take(w_v.at[k], vr)
    for h in range(2):
        lo = na * 32 + h * 8
        out[lo:lo + 8, :] = w_v[h, 0]
        out[lo + 16:lo + 24, :] = -w_v[h, 1]
        out[lo + 32:lo + 40, :] = w_v[h, 2]

    take(pf.at[pl.ds(0, (nr - 1) * f1)], s1)
    take(pg.at[pl.ds(0, (nr - 1) * f2)], s1)
    take(st.at[:, pl.ds(0, nc - 1)], bs)
    take(cw.at[:, :, 0], cs)
    take(cw.at[:, 0, 0], zxs)
    take(rp.at[pl.ds(0, 3)], rs_)
    take(fb, r1s)
    take(hop, r2s)
    take(zin, zs)
    take(wq.at[:, :, pl.ds(0, SIDE - 1)], ws)
    take(rb.at[:, pl.ds(0, nc - 1)], ts)
    take(rx, es)
    take(q_v.at[:, pl.ds(0, nc - 1)], qs)
    take(u_v.at[:, pl.ds(0, nz - 1)], us)
    take(w_v.at[0], vs)


def spread_fits(n, ids1, ids2, out):
    lane = lax.broadcasted_iota(jnp.int32, (8, 128), 1)
    bad = jnp.zeros((8, 128), F32)
    for ids, most in ((ids1, TIGHT[0]), (ids2, TIGHT[1])):
        count = jnp.zeros((8, 128), F32)
        for j in range(ids.shape[0]):
            count = count + jnp.where(lane == lax.rem(ids[j], n), 1.0, 0.0)
        bad = jnp.maximum(bad, count - most)
    out[0] = jnp.where(jnp.max(bad) > 0.5, 0, 1)


def part_out(rows, o, p1, p2, g1, g2, g3):
    p1[...] = o[0:rows, :]
    p2[...] = o[rows:2 * rows, :]
    for n, g in enumerate((g1, g2, g3)):
        g[...] = o[2 * rows + 16 * n:2 * rows + 16 * n + 16, :]


def fused(n1, n2, ident, struct_first, struct_second, inverse, factor_first, factor_second, link_factor, dinv_first, dinv_second):
    nr = lax.axis_size("row")
    nc = lax.axis_size("col")
    na, ns, ext, _ = inverse.shape
    f1, f2 = factor_first.shape[0], factor_second.shape[0]
    assert nr == nc == SIDE * SIDE and na == ns and na * nc <= 128 and n1 <= 8
    nu = n1 + n2
    nz = nr // 2
    width = -(-nu * 16 // 128) * 128
    deep = -(-n1 * 16 // 128) * 128
    rows = na * 16
    any_spec = pl.BlockSpec(memory_space=pl.ANY)
    vm = lambda *s: pltpu.VMEM(s, F32)
    dma = pltpu.SemaphoreType.DMA
    half = SIDE // 2
    return pl.pallas_call(
        functools.partial(kernel, nr, nc, na, ns, f1, f2, n1, n2, width),
        out_shape=jax.ShapeDtypeStruct((2 * rows + 48, 256), F32),
        in_specs=[pl.BlockSpec(memory_space=pltpu.SMEM)] * 2 + [any_spec] * 6,
        out_specs=pl.BlockSpec(memory_space=pltpu.VMEM),
        scratch_shapes=[
            pltpu.VMEM((32, 128), jnp.int32), pltpu.SMEM((32, 128), jnp.int32),
            vm(na, ns, 256, 256), vm(256, 256), vm(256, 256), vm(256, 256), vm(256, 256),
            vm(nr * f1, 8, 128), vm(nr * f2, 8, 128), vm(4, nu, 8, 128), vm(4, nu, 8, 128),
            vm(nu, nc, 8, 128), vm(nu, 2, 2, nc, 8, 128),
            pltpu.VMEM((n1, n1, 256, 512), BF16), pltpu.VMEM((nu, 768, 256), BF16),
            vm(nu, 2, SIDE, SIDE, 8, 256),
            vm(2, 2, nu, half, 8, 256), vm(2, 2, nu, half, 8, 256),
            vm(2, 2, nu, SIDE, 8, 256), vm(2, nu, SIDE, 8, 256),
            vm(2, nu, SIDE - 1, 8, 256),
            vm(deep, 256), vm(deep, 256), vm(2, nu, SIDE, 8, 256),
            vm(nc, 2, 8, width), vm(2, nc, 8, width),
            vm(3, nc, 2, 8, 256), vm(3, nc, 8, 256), vm(3, nc, 8, 256), vm(3, nc, 8, 256),
            vm(3, 8, 256), vm(3, nz, 8, 256), vm(2, 3, 8, 256),
            dma((ns,)), dma((3,)), dma, dma, dma, dma, dma, dma,
            dma, dma((nu,)), dma, dma((nu,)), dma, dma((nu,)),
            dma, dma((2, 2, nu)), dma, dma((2, 2, nu)), dma, dma((2, nu)),
            dma, dma, dma, dma, dma, dma((3,)), dma, dma((3,)), dma, dma((3,)), dma, dma,
        ],
        compiler_params=pltpu.CompilerParams(
            collective_id=ident, has_side_effects=True, vmem_limit_bytes=56 * 1024 * 1024
        ),
    )(struct_first, struct_second, inverse, factor_first, factor_second, link_factor, dinv_first, dinv_second)


def body(inverse, struct_first, struct_second, factor_first, factor_second, link_factor, dinv_first, dinv_second):
    na, _, ns, _, ext, _ = inverse.shape
    rows = na * 16
    args = (
        struct_first, struct_second, inverse.reshape(na, ns, ext, ext),
        factor_first, factor_second, link_factor, dinv_first, dinv_second,
    )
    roomy = lambda *v: fused(na, na, 0, *v)
    tight = lambda *v: fused(TIGHT[0], TIGHT[1], 1, *v)
    fits = pl.pallas_call(
        functools.partial(spread_fits, lax.axis_size("row")),
        out_shape=jax.ShapeDtypeStruct((1,), jnp.int32),
        in_specs=[pl.BlockSpec(memory_space=pltpu.SMEM)] * 2,
        out_specs=pl.BlockSpec(memory_space=pltpu.SMEM),
    )(struct_first, struct_second)
    o = lax.cond(fits[0] > 0, tight, roomy, *args)
    small = jax.ShapeDtypeStruct((16, 256), F32)
    tall = jax.ShapeDtypeStruct((rows, 256), F32)
    p1, p2, g1, g2, g3 = pl.pallas_call(
        functools.partial(part_out, rows),
        out_shape=(tall, tall, small, small, small),
    )(o)
    panel = lambda v: jnp.swapaxes(v.reshape(na, 1, 16, 256), 2, 3)
    turn = lambda v: jnp.swapaxes(v, 0, 1)
    return (panel(p1), turn(g1), panel(p2), turn(g2), turn(g3))


def solution(mesh):
    placed = (
        P(None, "row", None, "col", None, None),
        P(),
        P(),
        P("row", None, None),
        P("row", None, None),
        P(),
        P(),
        P(),
    )
    return jax.shard_map(
        body,
        mesh=mesh,
        in_specs=placed,
        out_specs=(
            P(None, "row", None, "col"),
            P(None, "col"),
            P(None, "row", None, "col"),
            P(None, "col"),
            P(None, "col"),
        ),
        check_vma=False,
    )
```

```python
import functools

import jax
import jax.numpy as jnp
from jax import lax
from jax.experimental import pallas as pl
from jax.experimental.pallas import tpu as pltpu
from jax.sharding import PartitionSpec as P

MESH = pl.DeviceIdType.MESH
SIDE = 4
TIGHT = (4, 3)
HAND_LAG = 3
USE_LAG = 5
F32 = jnp.float32
BF16 = jnp.bfloat16


def split(v):
    hi = v.astype(BF16)
    return hi, (v - hi.astype(F32)).astype(BF16)


def mm(p, q):
    return jnp.dot(p, q, preferred_element_type=F32)


def dot3(p, q):
    ph, plo = split(p)
    qh, qlo = split(q)
    return mm(ph, qh) + (mm(ph, qlo) + mm(plo, qh))


def kernel(
    nr, nc, na, ns, f1, f2, n1, n2, width,
    ids1, ids2, inv, fac1, fac2, link, dinv1, dinv2,
    out,
    tab_v, tab, a_v, l_v, d1_v, d2_v, lt_v,
    pf, pg, rps, rp, st, cw, lhs, w3, acc,
    hop, hopped, fb, ysum, zin, x1b, x2b, wq,
    st2, rb, m_v, rx, n_v, q_v, s_v, u_v, w_v,
    ld, lds, lt, s1, pfr, pgr, rs_, rr, bs, br, zxs, zxr, cs, cr,
    r1s, r1r, r2s, fbr, zs, zr, ws, wr, ts, tr, es, er, qs, qr, us, ur, vs, vr,
):
    r = lax.axis_index("row")
    c = lax.axis_index("col")
    k = lax.rem(r, 2)
    z = r // 2
    nz = nr // 2
    y = c // SIDE
    x = lax.rem(c, SIDE)
    e = lax.rem(z, 2)
    mate = z * 2 + (1 - k)
    z_up = lax.rem(z + 1, nz) * 2 + k
    z_down = lax.rem(z + nz - 1, nz) * 2 + k
    lanes = pl.multiple_of(128 * e, 128)
    nu = n1 + n2
    row1, row2, rowi, rowp, rowq = 0, 8, 16, 24, 25

    def remote(src, dst, ss, rs, row, col):
        return pltpu.make_async_remote_copy(
            src_ref=src, dst_ref=dst, send_sem=ss, recv_sem=rs,
            device_id=(row, col), device_id_type=MESH,
        )

    def row_at(i):
        step = (i + 1) // 2
        return lax.rem(r + nr // 2 + jnp.where(lax.rem(i, 2) == 1, step, -step), nr)

    def z_at(i):
        step = (i + 1) // 2
        return lax.rem(z + nz // 2 + jnp.where(lax.rem(i, 2) == 1, step, -step), nz)

    plane = sorted(
        ((dy, dx) for dy in range(SIDE) for dx in range(SIDE) if dy or dx),
        key=lambda v: -(min(v[0], SIDE - v[0]) + min(v[1], SIDE - v[1])),
    )

    def plane_cols():
        return [lax.rem(y + dy, SIDE) * SIDE + lax.rem(x + dx, SIDE) for dy, dx in plane]

    def take(ref, sem):
        pltpu.make_async_copy(ref, ref, sem).wait()

    def load_a(b):
        return pltpu.make_async_copy(inv.at[:, b], a_v.at[:, b], ld.at[b])

    small = [
        pltpu.make_async_copy(link, l_v, lds.at[0]),
        pltpu.make_async_copy(dinv1, d1_v, lds.at[1]),
        pltpu.make_async_copy(dinv2, d2_v, lds.at[2]),
    ]
    barrier = pltpu.get_barrier_semaphore()

    def greet_row(d, carry):
        pl.semaphore_signal(barrier, inc=1, device_id=(lax.rem(r + d, nr), c), device_id_type=MESH)
        return carry

    def greet_col(d, carry):
        pl.semaphore_signal(barrier, inc=1, device_id=(r, lax.rem(c + d, nc)), device_id_type=MESH)
        return carry

    lax.fori_loop(1, nr, greet_row, 0)
    lax.fori_loop(1, nc, greet_col, 0)
    row8 = pl.multiple_of(128 * k + 8 * c, 8)
    pltpu.make_async_copy(fac1.at[:, pl.ds(row8, 8), pl.ds(lanes, 128)], pf.at[pl.ds(r * f1, f1)], pfr).start()
    pltpu.make_async_copy(fac2.at[:, pl.ds(row8, 8), pl.ds(lanes, 128)], pg.at[pl.ds(r * f2, f2)], pgr).start()
    for cp in small:
        cp.start()
    for b in range(ns):
        load_a(b).start()
    pl.semaphore_wait(barrier, nr + nc - 2)

    def send_pieces(fac, buf, count, rsem):
        def go(d, carry):
            r2 = row_at(d)
            k2 = lax.rem(r2, 2)
            rows = pl.multiple_of(128 * k2 + 8 * c, 8)
            side = pl.multiple_of(128 * lax.rem(r2 // 2, 2), 128)
            remote(
                fac.at[:, pl.ds(rows, 8), pl.ds(side, 128)], buf.at[pl.ds(r * count, count)], s1, rsem, r2, c
            ).start()
            return carry

        lax.fori_loop(0, nr - 1, go, 0)

    send_pieces(fac1, pf, f1, pfr)
    send_pieces(fac2, pg, f2, pgr)

    tile = lax.broadcasted_iota(jnp.int32, (8, 128), 1)
    at1 = jnp.zeros((8, 128), jnp.int32)
    at2 = jnp.zeros((8, 128), jnp.int32)
    for j in range(ids1.shape[0]):
        at1 = jnp.where(tile == ids1[j], j + 1, at1)
    for j in range(ids2.shape[0]):
        at2 = jnp.where(tile == ids2[j], j + 1, at2)
    in2 = jnp.where(at2 > 0, 1, 0)
    only1 = jnp.where(at1 > 0, 1, 0) - in2

    def lower(v):
        tot = jnp.zeros_like(v)
        for d in range(1, na):
            tot = tot + jnp.where(tile >= d * nc, pltpu.roll(v, d * nc, axis=1), 0)
        return tot

    def fold_tiles(v):
        tot = v
        for d in range(1, na):
            tot = tot + pltpu.roll(v, 128 - d * nc, axis=1)
        return tot

    def spread(v):
        tot = v
        for d in range(1, na):
            tot = tot + jnp.where(tile >= d * nc, pltpu.roll(v, d * nc, axis=1), 0)
        return tot

    count2 = spread(jnp.where(tile < nc, fold_tiles(in2), 0))
    rank = jnp.where(in2 > 0, lower(in2), count2 + lower(only1))
    line = lax.broadcasted_iota(jnp.int32, (8, 128), 0)
    t1 = jnp.zeros((8, 128), jnp.int32)
    t2 = jnp.zeros((8, 128), jnp.int32)
    ti = jnp.zeros((8, 128), jnp.int32)
    for a in range(n1):
        hit = jnp.logical_and(at1 > 0, rank == a)
        t1 = jnp.where(line == a, fold_tiles(jnp.where(hit, at1, 0)), t1)
        t2 = jnp.where(line == a, fold_tiles(jnp.where(hit, at2, 0)), t2)
        ti = jnp.where(line == a, fold_tiles(jnp.where(hit, tile // nc, 0)), ti)
    tab_v[0:8, :] = t1 - 1
    tab_v[8:16, :] = t2 - 1
    tab_v[16:24, :] = ti
    tab_v[24:32, :] = jnp.where(
        line == 0, jnp.where(at1 > 0, rank, -1), jnp.where(in2 > 0, rank, -1)
    )
    to_smem = pltpu.make_async_copy(tab_v, tab, lt)
    to_smem.start()
    for cp in small:
        cp.wait()
    first = jnp.where(jnp.logical_and(r == 0, c == 0), 1.0, 0.0).astype(F32)
    lt_v[...] = jnp.transpose(l_v[...])
    d1_v[...] = jnp.transpose(d1_v[...]) * first
    d2_v[...] = jnp.transpose(d2_v[...]) * first

    to_smem.wait()
    take(pf, pfr)

    def pack(fg):
        def unit(b, carry):
            u = n1 * fg + b

            def one(c2, carry2):
                j = tab[(row1, row2)[fg] + b, c2]
                v = (pf, pg)[fg][jnp.maximum(j, 0)]
                st[u, c2] = jnp.where(j >= 0, v, 0.0)
                return carry2

            lax.fori_loop(0, nc, one, 0)
            pltpu.make_async_copy(st.at[u, c], cw.at[u, e, k, c], br.at[u]).start()

            for c2 in plane_cols():
                remote(st.at[u, c2], cw.at[u, e, k, c], bs, br.at[u], r, c2).start()
            return carry

        lax.fori_loop(0, (n1, n2)[fg], unit, 0)

    pack(0)
    take(pg, pgr)
    pack(1)

    other = z + 1 - 2 * e
    for t in range(4):
        z2 = z if t < 2 else other
        k2 = k if t % 2 == 0 else 1 - k
        r2 = z2 * 2 + k2
        for a in range(n1):
            j1 = tab[row1 + a, r2]
            rps[t, a] = jnp.where(j1 >= 0, pf[jnp.maximum(j1, 0)], 0.0)
        for a in range(n2):
            j2 = tab[row2 + a, r2]
            rps[t, n1 + a] = jnp.where(j2 >= 0, pg[jnp.maximum(j2, 0)], 0.0)
        if t == 0:
            pltpu.make_async_copy(rps.at[t], rp.at[e * 2 + k], rr).start()
        else:
            remote(rps.at[t], rp.at[e * 2 + k], rs_, rr, r2, c).start()

    def ring(h):
        if h == 0:
            return x, y * SIDE + lax.rem(x + 1, SIDE), y * SIDE + lax.rem(x + SIDE - 1, SIDE)
        return y, lax.rem(y + 1, SIDE) * SIDE + x, lax.rem(y + SIDE - 1, SIDE) * SIDE + x

    half = SIDE // 2

    def part(a, h, who, lo, n):
        if h == 0:
            return acc.at[a, 0, pl.ds(lo, n), who]
        return acc.at[a, 1, who, pl.ds(lo, n)]

    def step_one(a):
        for h in range(2):
            u, right, left = ring(h)
            up, down, far = lax.rem(u + 1, SIDE), lax.rem(u + SIDE - 1, SIDE), lax.rem(u + 2, SIDE)
            remote(part(a, h, far, 0, half), hop.at[h, 0, a], r1s, r1r.at[h, 0, a], r, right).start()
            remote(part(a, h, far, half, half), hop.at[h, 1, a], r1s, r1r.at[h, 1, a], r, left).start()
            remote(
                part(a, h, up, half, half), fb.at[h, 0, a, pl.ds(half, half)], r1s, fbr.at[h, 0, a], r, right
            ).start()
            remote(
                part(a, h, down, 0, half), fb.at[h, 1, a, pl.ds(0, half)], r1s, fbr.at[h, 1, a], r, left
            ).start()

    def weights(u):
        ff = jnp.concatenate([cw[u, 0].reshape(256, 128), cw[u, 1].reshape(256, 128)], axis=1)
        fh, fl = split(ff)
        w3[u, 0:256] = fh
        w3[u, 256:512] = fl
        w3[u, 512:768] = fh

    def term(fg, a, b):
        v = lhs[b, a]
        return mm(jnp.concatenate([v[:, 0:256], v[:, 0:256], v[:, 256:512]], axis=1), w3[n1 * fg + b])

    def shaped(v):
        return v.reshape(2, SIDE, SIDE, 8, 256)

    def part_sums(fg, b):
        def one(a, carry):
            u = n1 * fg + a
            got = shaped(term(fg, a, b))
            if fg == 1:
                acc[u] += got
            else:

                @pl.when(b == 0)
                def _():
                    acc[u] = got

                @pl.when(b > 0)
                def _():
                    acc[u] += got

            return carry

        lax.fori_loop(0, (n1, n2)[fg], one, 0)

    def finish(fg):
        n = (n1, n2)[fg]

        def one(a, carry):
            u = n1 * fg + a
            acc[u] += shaped(term(fg, a, n - 2) + term(fg, a, n - 1))
            step_one(u)
            return carry

        lax.fori_loop(0, n, one, 0)

    def start_second(a, carry):
        acc[n1 + a] = shaped(-dot3(acc[a].reshape(256, 256), l_v[...]))
        return carry

    def step_two(a, carry):
        for h in range(2):
            u, right, left = ring(h)
            up, down = lax.rem(u + 1, SIDE), lax.rem(u + SIDE - 1, SIDE)
            take(hop.at[h, 0, a], r1r.at[h, 0, a])
            hopped[h, 0, a] = hop[h, 0, a] + part(a, h, up, 0, half)[...]
            remote(
                hopped.at[h, 0, a], fb.at[h, 0, a, pl.ds(0, half)], r2s, fbr.at[h, 0, a], r, right
            ).start()
            take(hop.at[h, 1, a], r1r.at[h, 1, a])
            hopped[h, 1, a] = hop[h, 1, a] + part(a, h, down, half, half)[...]
            remote(
                hopped.at[h, 1, a], fb.at[h, 1, a, pl.ds(half, half)], r2s, fbr.at[h, 1, a], r, left
            ).start()
        return carry

    def row_pieces():
        take(rp, rr)
        for h in range(2):
            v = y if h == 0 else x
            for u in range(nu):
                for g in range(2):
                    wq[h, u, v, :, g * 128:g * 128 + 128] = rp[g * 2 + h, u]
            for d in range(1, SIDE):
                v2 = lax.rem(v + d, SIDE)
                col = v2 * SIDE + x if h == 0 else y * SIDE + v2
                remote(wq.at[h, :, v], wq.at[h, :, v], ws, wr, r, col).start()

    def swap(u):
        mine = cw.at[u, e, k]
        take(mine, br.at[u])
        remote(mine, mine, cs, cr.at[u], mate, c).start()
        remote(mine, mine, zxs, zxr.at[u], jnp.where(lax.rem(u, 2) == 0, z_down, z_up), c).start()

    def hand(u):
        got = cw.at[u, 1 - e, k]
        take(got, zxr.at[u])
        remote(got, got, cs, cr.at[u], mate, c).start()

    def units(s, carry):
        @pl.when(s < nu)
        def _():
            swap(s)

        @pl.when(jnp.logical_and(s >= HAND_LAG, s < nu + HAND_LAG))
        def _():
            hand(s - HAND_LAG)

        @pl.when(s == USE_LAG - 1)
        def _():
            row_pieces()

        @pl.when(s >= USE_LAG)
        def _():
            u = s - USE_LAG
            take(cw.at[u, :, 1 - k], cr.at[u])
            weights(u)

            @pl.when(u < n1 - 2)
            def _():
                part_sums(0, u)

            @pl.when(u == n1 - 1)
            def _():
                finish(0)
                lax.fori_loop(0, n2, start_second, 0)

            @pl.when(jnp.logical_and(u >= n1, u < nu - 2))
            def _():
                part_sums(1, u - n1)

            @pl.when(u == nu - 1)
            def _():
                lax.fori_loop(0, n1, step_two, 0)
                finish(1)

        return carry

    for b in range(ns):
        load_a(b).wait()

    def cast(i, carry):
        a, b = i // n1, lax.rem(i, n1)
        ah, al = split(a_v[tab[rowi + a, r], tab[rowi + b, c]])
        lhs[b, a, :, 0:256] = ah
        lhs[b, a, :, 256:512] = al
        return carry

    lax.fori_loop(0, n1 * n1, cast, 0)
    lax.fori_loop(0, nu + USE_LAG, units, 0)


    def second(a, carry):
        for h in range(2):
            u = ring(h)[0]
            take(fb.at[h, 0, a], fbr.at[h, 0, a])
            take(fb.at[h, 1, a], fbr.at[h, 1, a])
            ysum[h, a] = part(a, h, u, 0, SIDE)[...] + (fb[h, 0, a] + fb[h, 1, a])
            v = y if h == 0 else x
            for d in range(1, SIDE):
                v2 = lax.rem(v + d, SIDE)
                col = v2 * SIDE + x if h == 0 else y * SIDE + v2
                remote(ysum.at[h, a, v2], zin.at[h, a, d - 1], zs, zr.at[h, a], r, col).start()
        return carry


    def gather(fg, buf):
        def one(a, carry):
            u = n1 * fg + a
            for h in range(2):
                v = y if h == 0 else x
                take(zin.at[h, u], zr.at[h, u])
                tot = ysum[h, u, v] + (zin[h, u, 0] + zin[h, u, 1] + zin[h, u, 2])
                buf[pl.ds(pl.multiple_of(a * 16 + h * 8, 8), 8), :] = tot
            return carry

        lax.fori_loop(0, (n1, n2)[fg], one, 0)

    def terms(fg):
        lo, n = ((0, n1), (n1, n2))[fg]
        return ysum[:, lo:lo + n].reshape(2 * n * SIDE * 8, 256)

    def own_rows(fg):
        lo, n = ((0, n1), (n1, n2))[fg]
        return wq[:, lo:lo + n].reshape(2 * n * SIDE * 8, 256)

    lax.fori_loop(0, n1, second, 0)
    take(wq.at[:, :, pl.ds(0, SIDE - 1)], wr)
    d1t = dot3(jnp.transpose(terms(0)), own_rows(0)) + d1_v[...]
    m_v[0] = d1t.reshape(nc, 2, 8, 256)
    common = ysum[:, 0:n2].reshape(2 * n2 * SIDE * 8, 256)
    jt = dot3(lt_v[...], d1t) - dot3(jnp.transpose(own_rows(1)), common)
    m_v[1] = jt.reshape(nc, 2, 8, 256)

    def fold(t):
        return remote(m_v.at[t, :, 1 - k], rx.at[t], es, er.at[t], mate, c)

    def send_term(t):
        take(rx.at[t], er.at[t])
        n_v[t] = m_v[t, :, k] + rx[t]
        pltpu.make_async_copy(n_v.at[t, c], q_v.at[t, c], qr.at[t]).start()

        for c2 in plane_cols():
            remote(n_v.at[t, c2], q_v.at[t, c], qs, qr.at[t], r, c2).start()

    fold(0).start()
    fold(1).start()
    lax.fori_loop(n1, nu, step_two, 0)
    base = dot3(jt, l_v[...]) + d2_v[...]
    send_term(0)
    send_term(1)
    lax.fori_loop(n1, nu, second, 0)
    et = dot3(jnp.transpose(terms(1)), own_rows(1)) + base
    m_v[2] = et.reshape(nc, 2, 8, 256)
    fold(2).start()

    send_term(2)

    gather(0, x1b)
    gather(1, x2b)

    lane = lax.broadcasted_iota(jnp.int32, (16, 128), 1) // 16
    for c2 in range(nc):
        blk, off = c2 // 8, c2 % 8
        for q in range(width // 128):
            val = jnp.zeros((16, 128), F32)
            for g in range(8):
                u = q * 8 + g
                if u < nu:
                    buf, a = (x1b, u) if u < n1 else (x2b, u - n1)
                    src = buf[a * 16:a * 16 + 16, blk * 128:blk * 128 + 128]
                    shift = (16 * (g - off)) % 128
                    if shift:
                        src = pltpu.roll(src, shift, axis=1)
                    val = jnp.where(lane == g, src, val)
            st2[c2, :, :, q * 128:(q + 1) * 128] = val.reshape(2, 8, 128)
    pltpu.make_async_copy(st2.at[c], rb.at[:, c], tr).start()

    def send_cols(d, carry):
        c2 = lax.rem(c + d, nc)
        remote(st2.at[c2], rb.at[:, c], ts, tr, r, c2).start()
        return carry

    lax.fori_loop(1, nc, send_cols, 0)

    def send_sum(t):
        take(q_v.at[t], qr.at[t])
        tot = q_v[t, 0]
        for i in range(1, nc):
            tot = tot + q_v[t, i]
        s_v[t] = tot
        pltpu.make_async_copy(s_v.at[t], u_v.at[t, z], ur.at[t]).start()

        def go(d, carry):
            z2 = z_at(d)
            remote(s_v.at[t], u_v.at[t, z], us, ur.at[t], z2 * 2 + k, c).start()
            return carry

        lax.fori_loop(0, nz - 1, go, 0)

    for t in range(3):
        send_sum(t)

    take(rb, tr)
    cols = jnp.transpose(rb[...].reshape(256, width))
    for fg in range(2):
        for a in range(na):
            slot_of = tab[(rowp, rowq)[fg], a * nr + r]
            val = jnp.zeros((16, 256), F32)
            for i in range((n1, n2)[fg]):
                lo = (n1 * fg + i) * 16
                val = jnp.where(slot_of == i, -cols[lo:lo + 16, :], val)
            lo = (na * fg + a) * 16
            out[lo:lo + 16, :] = val

    for t in range(3):
        take(u_v.at[t], ur.at[t])
        tot = u_v[t, 0]
        for i in range(1, nz):
            tot = tot + u_v[t, i]
        w_v[k, t] = tot
    last = remote(w_v.at[k], w_v.at[k], vs, vr, mate, c)
    last.start()
    take(w_v.at[k], vr)
    for h in range(2):
        lo = na * 32 + h * 8
        out[lo:lo + 8, :] = w_v[h, 0]
        out[lo + 16:lo + 24, :] = -w_v[h, 1]
        out[lo + 32:lo + 40, :] = w_v[h, 2]

    take(pf.at[pl.ds(0, (nr - 1) * f1)], s1)
    take(pg.at[pl.ds(0, (nr - 1) * f2)], s1)
    take(st.at[:, pl.ds(0, nc - 1)], bs)
    take(cw.at[:, :, 0], cs)
    take(cw.at[:, 0, 0], zxs)
    take(rp.at[pl.ds(0, 3)], rs_)
    take(fb, r1s)
    take(hop, r2s)
    take(zin, zs)
    take(wq.at[:, :, pl.ds(0, SIDE - 1)], ws)
    take(rb.at[:, pl.ds(0, nc - 1)], ts)
    take(rx, es)
    take(q_v.at[:, pl.ds(0, nc - 1)], qs)
    take(u_v.at[:, pl.ds(0, nz - 1)], us)
    take(w_v.at[0], vs)


def spread_fits(n, ids1, ids2, out):
    lane = lax.broadcasted_iota(jnp.int32, (8, 128), 1)
    bad = jnp.zeros((8, 128), F32)
    for ids, most in ((ids1, TIGHT[0]), (ids2, TIGHT[1])):
        count = jnp.zeros((8, 128), F32)
        for j in range(ids.shape[0]):
            count = count + jnp.where(lane == lax.rem(ids[j], n), 1.0, 0.0)
        bad = jnp.maximum(bad, count - most)
    out[0] = jnp.where(jnp.max(bad) > 0.5, 0, 1)


def part_out(rows, o, p1, p2, g1, g2, g3):
    p1[...] = o[0:rows, :]
    p2[...] = o[rows:2 * rows, :]
    for n, g in enumerate((g1, g2, g3)):
        g[...] = o[2 * rows + 16 * n:2 * rows + 16 * n + 16, :]


def fused(n1, n2, ident, struct_first, struct_second, inverse, factor_first, factor_second, link_factor, dinv_first, dinv_second):
    nr = lax.axis_size("row")
    nc = lax.axis_size("col")
    na, ns, ext, _ = inverse.shape
    f1, f2 = factor_first.shape[0], factor_second.shape[0]
    assert nr == nc == SIDE * SIDE and na == ns and na * nc <= 128 and n1 <= 8
    nu = n1 + n2
    nz = nr // 2
    width = -(-nu * 16 // 128) * 128
    deep = -(-n1 * 16 // 128) * 128
    rows = na * 16
    any_spec = pl.BlockSpec(memory_space=pl.ANY)
    vm = lambda *s: pltpu.VMEM(s, F32)
    dma = pltpu.SemaphoreType.DMA
    half = SIDE // 2
    return pl.pallas_call(
        functools.partial(kernel, nr, nc, na, ns, f1, f2, n1, n2, width),
        out_shape=jax.ShapeDtypeStruct((2 * rows + 48, 256), F32),
        in_specs=[pl.BlockSpec(memory_space=pltpu.SMEM)] * 2 + [any_spec] * 6,
        out_specs=pl.BlockSpec(memory_space=pltpu.VMEM),
        scratch_shapes=[
            pltpu.VMEM((32, 128), jnp.int32), pltpu.SMEM((32, 128), jnp.int32),
            vm(na, ns, 256, 256), vm(256, 256), vm(256, 256), vm(256, 256), vm(256, 256),
            vm(nr * f1, 8, 128), vm(nr * f2, 8, 128), vm(4, nu, 8, 128), vm(4, nu, 8, 128),
            vm(nu, nc, 8, 128), vm(nu, 2, 2, nc, 8, 128),
            pltpu.VMEM((n1, n1, 256, 512), BF16), pltpu.VMEM((nu, 768, 256), BF16),
            vm(nu, 2, SIDE, SIDE, 8, 256),
            vm(2, 2, nu, half, 8, 256), vm(2, 2, nu, half, 8, 256),
            vm(2, 2, nu, SIDE, 8, 256), vm(2, nu, SIDE, 8, 256),
            vm(2, nu, SIDE - 1, 8, 256),
            vm(deep, 256), vm(deep, 256), vm(2, nu, SIDE, 8, 256),
            vm(nc, 2, 8, width), vm(2, nc, 8, width),
            vm(3, nc, 2, 8, 256), vm(3, nc, 8, 256), vm(3, nc, 8, 256), vm(3, nc, 8, 256),
            vm(3, 8, 256), vm(3, nz, 8, 256), vm(2, 3, 8, 256),
            dma((ns,)), dma((3,)), dma, dma, dma, dma, dma, dma,
            dma, dma((nu,)), dma, dma((nu,)), dma, dma((nu,)),
            dma, dma((2, 2, nu)), dma, dma((2, 2, nu)), dma, dma((2, nu)),
            dma, dma, dma, dma, dma, dma((3,)), dma, dma((3,)), dma, dma((3,)), dma, dma,
        ],
        compiler_params=pltpu.CompilerParams(
            collective_id=ident, has_side_effects=True, vmem_limit_bytes=56 * 1024 * 1024
        ),
    )(struct_first, struct_second, inverse, factor_first, factor_second, link_factor, dinv_first, dinv_second)


def body(inverse, struct_first, struct_second, factor_first, factor_second, link_factor, dinv_first, dinv_second):
    na, _, ns, _, ext, _ = inverse.shape
    rows = na * 16
    args = (
        struct_first, struct_second, inverse.reshape(na, ns, ext, ext),
        factor_first, factor_second, link_factor, dinv_first, dinv_second,
    )
    roomy = lambda *v: fused(na, na, 0, *v)
    tight = lambda *v: fused(TIGHT[0], TIGHT[1], 1, *v)
    fits = pl.pallas_call(
        functools.partial(spread_fits, lax.axis_size("row")),
        out_shape=jax.ShapeDtypeStruct((1,), jnp.int32),
        in_specs=[pl.BlockSpec(memory_space=pltpu.SMEM)] * 2,
        out_specs=pl.BlockSpec(memory_space=pltpu.SMEM),
    )(struct_first, struct_second)
    o = lax.cond(fits[0] > 0, tight, roomy, *args)
    small = jax.ShapeDtypeStruct((16, 256), F32)
    tall = jax.ShapeDtypeStruct((rows, 256), F32)
    p1, p2, g1, g2, g3 = pl.pallas_call(
        functools.partial(part_out, rows),
        out_shape=(tall, tall, small, small, small),
    )(o)
    panel = lambda v: jnp.swapaxes(v.reshape(na, 1, 16, 256), 2, 3)
    turn = lambda v: jnp.swapaxes(v, 0, 1)
    return (panel(p1), turn(g1), panel(p2), turn(g2), turn(g3))


def solution(mesh):
    placed = (
        P(None, "row", None, "col", None, None),
        P(),
        P(),
        P("row", None, None),
        P("row", None, None),
        P(),
        P(),
        P(),
    )
    return jax.shard_map(
        body,
        mesh=mesh,
        in_specs=placed,
        out_specs=(
            P(None, "row", None, "col"),
            P(None, "col"),
            P(None, "row", None, "col"),
            P(None, "col"),
            P(None, "col"),
        ),
        check_vma=False,
    )
```
